1024 devices in a mesh: expert: 64 (over x, y), hidden: 16 (over z, core).
Axes of the slice: x: 8, y: 8, z: 8, core: 2. Of those that a mesh axis runs over, the one named last changes fastest.
Arguments:
- tokens: bfloat16 [16, 128, 2048], P('hidden', 'expert'), may hold values from -6 to 6
- grad_out: bfloat16 [16, 128, 2048], P('hidden', 'expert'), may hold values from -6 to 6
- expert_ids: int32 [16, 128, 8], P('hidden', 'expert'), may hold values from 0 to 63, all different within a row; in each aligned block of 128 rows (0 to 127, 128 to 255, ..., all dimensions but the last counted through in order) at most 32 rows name the same one
- router_logits: float32 [16, 128, 8], P('hidden', 'expert'), may hold values from -4 to 4
- w_gate: bfloat16 [64, 2048, 1536], P('expert', None, 'hidden'), may hold values from -0.125 to 0.125
- w_up: bfloat16 [64, 2048, 1536], P('expert', None, 'hidden'), may hold values from -0.125 to 0.125
- w_down: bfloat16 [64, 1536, 2048], P('expert', 'hidden'), may hold values from -0.15625 to 0.15625
Outputs:
- grad_in: float32 [16, 128, 2048], P('hidden', 'expert')
- grad_logits: float32 [16, 128, 8], P('hidden', 'expert')
- grad_gate: float32 [64, 2048, 1536], P('expert', None, 'hidden')
- grad_up: float32 [64, 2048, 1536], P('expert', None, 'hidden')
- grad_down: float32 [64, 1536, 2048], P('expert', 'hidden')
The draws below stay inside these ranges and needn't reach their ends.
Inputs may be any that keep to these rules, and one draw needn't show every extreme that they name: `expert_ids`: each token names 8 different experts. Among the tokens of one hidden index no expert is named more than 32 times, a bound that some block reaches.
All inputs are finite; a program needn't handle non-finite values.
Results may differ from the reference program's by a relative error of at most 0.0041.
Values may be sent and summed in bfloat16 or wider, within the bound.
A program may use at most 32 MiB of HBM per device.

```python
import math
import jax
import jax.numpy as jnp
import numpy as np
from jax import lax

D = 2048
FF = 1536
TOP = 8
EXPERTS = 64
TOK_SL = 128
CAP = 32
N_HIDDEN = 16


def levels(key, dims, shards, smallest, top_value):
    gain, own = 1.0, jax.random.fold_in(key, 6)
    for axis_at, parts in shards:
        heights = jnp.exp(jax.random.uniform(jax.random.fold_in(own, axis_at), (parts,), jnp.float32, smallest / len(shards), top_value / len(shards)))
        gain = gain * jnp.repeat(heights, dims[axis_at] // parts).reshape([-1 if axis == axis_at else 1 for axis in range(len(dims))])
    return gain


def assign_block(key, own, number, rows, count, top, most, skew):
    order = jax.random.permutation(key, count)
    packed, usual = portions_of(count, rows * top, most, skew, True), portions_of(count, rows * top, most, skew, False)
    places = jnp.arange(count)

    def named(lengths, offset_by):
        used = int((lengths > 0).sum())
        fixed = max(1, used // 4)
        passed = fixed + (places - fixed + offset_by * (used - fixed)) % max(1, count - fixed)
        return jnp.zeros((count,), jnp.int32).at[order[jnp.where(places < fixed, places, passed)]].set(jnp.asarray(lengths, jnp.int32))

    lengths = jnp.where(number % 4 == 0, named(packed, number // 4), named(usual, number - number // 4 - 1))
    mixed = jax.random.permutation(jax.random.fold_in(own, 3), count)
    donor, taker = mixed[0:count // 2 * 2:2], mixed[1:count // 2 * 2:2]
    margin = jnp.minimum(lengths[donor] - 1, most - lengths[taker]) // 2
    margin = jnp.where((donor == order[0]) | (taker == order[0]) | (lengths[taker] == 0), 0, jnp.maximum(margin, 0))
    passed = jax.random.randint(jax.random.fold_in(own, 4), (count // 2,), 0, 1 << 20) % (margin + 1)
    lengths = lengths.at[donor].add(-passed).at[taker].add(passed)
    labels = jnp.searchsorted(jnp.cumsum(lengths), jnp.arange(rows * top), side="right").astype(jnp.int32)
    table = labels.reshape(top, rows).T
    table = table[jax.random.permutation(jax.random.fold_in(own, 1), rows)]
    offset_by = jax.random.randint(jax.random.fold_in(own, 2), (rows, 1), 0, top)
    return jnp.take_along_axis(table, (jnp.arange(top)[None, :] + offset_by) % top, axis=1)


def portions_of(count, total, limit, skew, full):
    loads = [(1 << 20) // math.isqrt(standing ** skew) + 1 for standing in range(1, count + 1)]
    largest = limit if full else min(limit, max(-(-total // count), total * loads[0] // sum(loads)))
    least = 1 if total - largest >= count - 1 else 0
    given, surplus = [largest] + [least] * (count - 1), total - largest - least * (count - 1)
    while surplus > 0:
        movable = [i for i in range(1, count) if given[i] < largest] or [i for i in range(1, count) if given[i] < limit]
        pool, remaining = sum([loads[i] for i in movable]), surplus
        for i in movable:
            more = min(limit - given[i], max(1, remaining * loads[i] // pool), surplus)
            given[i] = given[i] + more
            surplus = surplus - more
    return np.array(given)


def noise(key, shape, deviation, most, pieces=(), kind=jnp.bfloat16):
    entries = deviation * jax.random.normal(key, shape, jnp.float32)
    if pieces:
        entries = entries * levels(key, shape, pieces, -0.22, 0.18)
    return jnp.clip(entries, -most, most).astype(kind)


def setup_inputs(seed: int = 0) -> dict:
    key_of = jax.random.split(jax.random.key(seed), 8)
    tokens = noise(key_of[0], (N_HIDDEN, TOK_SL, D), 1.0, 6.0, ((0, 16), (1, 64)))
    grad_out = noise(key_of[1], (N_HIDDEN, TOK_SL, D), 1.0, 6.0, ((0, 16), (1, 64)))
    expert_ids_keys = jax.random.split(jax.random.fold_in(key_of[2], 1), N_HIDDEN * TOK_SL // TOK_SL)
    expert_ids_turns = jax.random.permutation(jax.random.fold_in(key_of[2], 3), N_HIDDEN * TOK_SL // TOK_SL)
    expert_ids = jax.vmap(lambda own, number: assign_block(jax.random.fold_in(key_of[2], 2), own, number, TOK_SL, EXPERTS, TOP, CAP, 2))(expert_ids_keys, expert_ids_turns).reshape((N_HIDDEN, TOK_SL, TOP))
    router_logits = noise(key_of[3], (N_HIDDEN, TOK_SL, TOP), 1.0, 4.0, ((0, 16), (1, 64)), jnp.float32)
    w_gate = noise(key_of[4], (EXPERTS, D, FF), D ** -0.5, 0.125, ((0, 64), (2, 16)))
    w_up = noise(key_of[5], (EXPERTS, D, FF), D ** -0.5, 0.125, ((0, 64), (2, 16)))
    w_down = noise(key_of[6], (EXPERTS, FF, D), FF ** -0.5, 0.15625, ((0, 64), (1, 16)))
    return {"tokens": tokens, "grad_out": grad_out, "expert_ids": expert_ids, "router_logits": router_logits, "w_gate": w_gate, "w_up": w_up, "w_down": w_down}


def expert_grads(x_rows, grad_rows, gate_col, gate_weight, up_weight, down_weight):
    pre_gate = jnp.dot(x_rows, gate_weight, preferred_element_type=jnp.float32)
    pre_up = jnp.dot(x_rows, up_weight, preferred_element_type=jnp.float32)
    back_grad = lax.dot_general(grad_rows, down_weight, (((1,), (1,)), ((), ())), preferred_element_type=jnp.float32)
    sigmoid_gate = jax.nn.sigmoid(pre_gate)
    silu_gate = pre_gate * sigmoid_gate
    active = silu_gate * pre_up
    gate_grad = jnp.sum(active * back_grad, axis=-1)
    weight = gate_col.astype(jnp.float32)
    scaled = (weight * active).astype(jnp.bfloat16)
    weighted_back = weight * back_grad
    d_gate_pre = (weighted_back * pre_up * sigmoid_gate * (1.0 + pre_gate * (1.0 - sigmoid_gate))).astype(jnp.bfloat16)
    d_up_pre = (weighted_back * silu_gate).astype(jnp.bfloat16)
    row_grad = lax.dot_general(d_gate_pre, gate_weight, (((1,), (1,)), ((), ())), preferred_element_type=jnp.float32)
    row_grad = row_grad + lax.dot_general(d_up_pre, up_weight, (((1,), (1,)), ((), ())), preferred_element_type=jnp.float32)
    sum_gate = lax.dot_general(x_rows, d_gate_pre, (((0,), (0,)), ((), ())), preferred_element_type=jnp.float32)
    sum_up = lax.dot_general(x_rows, d_up_pre, (((0,), (0,)), ((), ())), preferred_element_type=jnp.float32)
    sum_down = lax.dot_general(scaled, grad_rows, (((0,), (0,)), ((), ())), preferred_element_type=jnp.float32)
    return row_grad, gate_grad, sum_gate, sum_up, sum_down


def reference(tokens, grad_out, expert_ids, router_logits, w_gate, w_up, w_down):
    highest = lax.Precision.HIGHEST
    raised = jnp.exp(router_logits)
    gate_probs = raised / jnp.sum(raised, axis=-1, keepdims=True)
    gate_rows = gate_probs.astype(jnp.bfloat16)
    tokens_wide = tokens.astype(jnp.float32)
    grads_wide = grad_out.astype(jnp.float32)
    positions = jnp.arange(CAP, dtype=jnp.int32)

    def per_expert(totals, expert):
        input_acc, logit_acc = totals
        chosen = expert_ids == expert
        column = jnp.sum(jnp.where(chosen, gate_rows.astype(jnp.float32), jnp.float32(0.0)), axis=-1)
        picked = jnp.any(chosen, axis=-1)
        row_order = jnp.cumsum(picked.astype(jnp.int32), axis=1) - 1
        placing = ((row_order[:, None, :] == positions[None, :, None]) & picked[:, None, :]).astype(jnp.float32)
        x_rows = jnp.einsum("hct,htd->hcd", placing, tokens_wide, precision=highest).astype(jnp.bfloat16).reshape(N_HIDDEN * CAP, D)
        grad_rows = jnp.einsum("hct,htd->hcd", placing, grads_wide, precision=highest).astype(jnp.bfloat16).reshape(N_HIDDEN * CAP, D)
        gate_col = jnp.einsum("hct,ht->hc", placing, column, precision=highest).reshape(N_HIDDEN * CAP, 1)
        gate_weight = lax.dynamic_index_in_dim(w_gate, expert, 0, keepdims=False)
        up_weight = lax.dynamic_index_in_dim(w_up, expert, 0, keepdims=False)
        down_weight = lax.dynamic_index_in_dim(w_down, expert, 0, keepdims=False)
        row_grad, gate_grad, sum_gate, sum_up, sum_down = expert_grads(x_rows, grad_rows, gate_col, gate_weight, up_weight, down_weight)
        input_acc = input_acc + jnp.einsum("hct,hcd->htd", placing, row_grad.reshape(N_HIDDEN, CAP, D), precision=highest)
        token_gate = jnp.einsum("hct,hc->ht", placing, gate_grad.reshape(N_HIDDEN, CAP), precision=highest)
        logit_acc = logit_acc + jnp.where(chosen, token_gate[:, :, None], jnp.float32(0.0))
        return (input_acc, logit_acc), (sum_gate, sum_up, sum_down)

    start_state = (jnp.zeros((N_HIDDEN, TOK_SL, D), jnp.float32), jnp.zeros((N_HIDDEN, TOK_SL, TOP), jnp.float32))
    finals, stacked = lax.scan(per_expert, start_state, jnp.arange(EXPERTS, dtype=jnp.int32))
    input_acc, gate_grad = finals
    grad_logits = gate_probs * (gate_grad - jnp.sum(gate_probs * gate_grad, axis=-1, keepdims=True))
    return input_acc, grad_logits, stacked[0], stacked[1], stacked[2]
```

```python
import functools
import math

import jax
import jax.numpy as jnp
from jax import lax
from jax.experimental import pallas as pl
from jax.experimental.pallas import tpu as pltpu
from jax.sharding import PartitionSpec as P

MESH = pl.DeviceIdType.MESH
CAP = 32
LANES = 128
F32 = jnp.float32
BF16 = jnp.bfloat16


def split(value):
    lane = lax.broadcasted_iota(jnp.int32, value.shape, value.ndim - 1)
    high = value.astype(BF16).astype(F32)
    return jnp.where(lane < LANES // 2, high, value - high).astype(BF16)


def join(parts):
    wide = parts.astype(F32)
    return wide + pltpu.roll(wide, LANES // 2, 1)


def kernel(
    nx, ny, nz,
    xin, gin, wgu, wd,
    out_in, out_gate_rows, out_gate, out_up, out_down,
    a1, b1, flat_a, flat_b, a2, b2, xall, gall, dcat, scaled_t, rfull, rhalf, sib,
    ring_send_lo, ring_recv_lo, ring_send_hi, ring_recv_hi,
    c1, c1r, e1, e1r, c2, c2r, e2, e2r,
    s1a, r1a, s1b, r1b, s2a, r2a, s2b, r2b,
    sxr, rxr, sxs, rxs, sgr, rgr, sgs, rgs,
    ss, rs, slo, rlo, shi, rhi,
    s3a, r3a, s3b, r3b, s4a, r4a, s4b, r4b,
):
    mine = lax.axis_index("expert")
    hid = lax.axis_index("hidden")
    mx, my = mine // ny, mine % ny
    mz, core = hid // 2, hid % 2
    dim = wd.shape[1]
    units = wd.shape[0]
    half = dim // 2
    tokens = 2 * nx * ny
    padded = dim + LANES

    def at_x(x):
        return {"expert": x * ny + my, "hidden": hid}

    def at_y(y):
        return {"expert": mx * ny + y, "hidden": hid}

    def at_z(z):
        return {"expert": mine, "hidden": 2 * z + core}

    sibling = {"expert": mine, "hidden": 2 * mz + 1 - core}
    up_z, down_z = (mz + 1) % nz, (mz + nz - 1) % nz
    pending = []

    def send(src, dst, send_sem, recv_sem, device):
        copy = pltpu.make_async_remote_copy(
            src_ref=src, dst_ref=dst, send_sem=send_sem, recv_sem=recv_sem,
            device_id=device, device_id_type=MESH,
        )
        copy.start()
        pending.append(copy)
        return copy

    barrier = pltpu.get_barrier_semaphore()
    greet = [at_x((mx + d) % nx) for d in range(1, nx)]
    greet += [at_y((my + d) % ny) for d in range(1, ny)]
    greet += [at_z(up_z), at_z(down_z), sibling]
    for device in greet:
        pl.semaphore_signal(barrier, inc=1, device_id=device, device_id_type=MESH)
    pl.semaphore_wait(barrier, len(greet))

    a_sends = [
        send(xin, a1.at[mx], s1a.at[d], r1a.at[d], at_x((mx + d) % nx)) for d in range(1, nx)
    ]
    b_sends = [
        send(gin, b1.at[my], s1b.at[d], r1b.at[d], at_y((my + d) % ny)) for d in range(1, ny)
    ]
    a1[mx] = xin[...]
    b1[my] = gin[...]
    for copy in a_sends:
        copy.wait_recv()
    for k in range(nx):
        flat_a[2 * k : 2 * k + 2, :] = a1[k].astype(F32)
    a2[my] = flat_a[...].astype(BF16)
    a_sends = [
        send(a2.at[my], a2.at[my], s2a.at[d], r2a.at[d], at_y((my + d) % ny)) for d in range(1, ny)
    ]
    for copy in b_sends:
        copy.wait_recv()
    for k in range(ny):
        flat_b[2 * k : 2 * k + 2, :] = b1[k].astype(F32)
    b2[mx] = flat_b[...].astype(BF16)
    b_sends = [
        send(b2.at[mx], b2.at[mx], s2b.at[d], r2b.at[d], at_x((mx + d) % nx)) for d in range(1, nx)
    ]

    lane = lax.broadcasted_iota(jnp.int32, (8, LANES), 1)
    own_lane = jnp.where(lane == mine, 1.0, 0.0).astype(BF16)

    def order_b(t):
        xx, yy, jj = t // (2 * ny), (t // 2) % ny, t % 2
        return (yy * nx + xx) * 2 + jj

    def placing_of(table, order):
        gate = lax.dot_general(own_lane, table, (((1,), (1,)), ((), ())), preferred_element_type=F32)
        picked = jnp.where(gate > 0.0, 1.0, 0.0)
        before = order(lax.broadcasted_iota(jnp.int32, (tokens, tokens), 0))
        after = order(lax.broadcasted_iota(jnp.int32, (tokens, tokens), 1))
        upto = jnp.where(before <= after, 1.0, 0.0).astype(BF16)
        rank = jnp.dot(picked.astype(BF16), upto, preferred_element_type=F32) - 1.0
        rank = jnp.where(picked > 0.0, rank, -1.0)
        slot = lax.broadcasted_iota(jnp.int32, (CAP, tokens), 0).astype(F32)
        return jnp.where(rank[0:1, :] == slot, 1.0, 0.0)

    for copy in a_sends:
        copy.wait_recv()
    all_a = a2[...].reshape(tokens, padded)
    place_a = placing_of(all_a[:, dim:], lambda t: t)
    xall[hid] = jnp.dot(place_a.astype(BF16), all_a, preferred_element_type=F32).astype(BF16)

    def ring_start(buf, sems, cross, up_hops):
        own = buf.at[hid]
        first = [
            send(own, own, sems[0].at[0, 0], sems[1].at[0, 0], at_z(up_z)),
            send(own, own, sems[0].at[1, 0], sems[1].at[1, 0], at_z(down_z)),
        ]
        over = [send(own, own, cross[0].at[0], cross[1].at[0], sibling)]
        return first, over

    def ring_step(buf, sems, cross, hops, state, step):
        waits, over = state
        for side, sign in ((0, 1), (1, -1)):
            if step >= hops[side]:
                continue
            waits[side].wait_recv()
            block = buf.at[2 * ((mz - sign * (step + 1) + nz) % nz) + core]
            if step + 1 < hops[side]:
                waits[side] = send(
                    block, block, sems[0].at[side, step + 1], sems[1].at[side, step + 1],
                    at_z(up_z if side == 0 else down_z),
                )
            number = 1 + 2 * step + side
            over.append(send(block, block, cross[0].at[number], cross[1].at[number], sibling))

    long, short = nz // 2, nz // 2 - 1
    x_state = ring_start(xall, (sxr, rxr), (sxs, rxs), long)
    for copy in b_sends:
        copy.wait_recv()
    all_b = b2[...].reshape(tokens, padded)
    place_b = placing_of(all_b[:, dim:], order_b)
    gall[hid] = jnp.dot(
        place_b.astype(BF16), all_b[:, :dim], preferred_element_type=F32
    ).astype(BF16)
    g_state = ring_start(gall, (sgr, rgr), (sgs, rgs), short)
    for step in range(long):
        ring_step(xall, (sxr, rxr), (sxs, rxs), (long, short), x_state, step)
        ring_step(gall, (sgr, rgr), (sgs, rgs), (short, long), g_state, step)
    for copy in x_state[1] + g_state[1]:
        copy.wait_recv()

    per = LANES // CAP

    def group(g, _):
        at = pl.ds(g * per, per)
        cols = pl.ds(pl.multiple_of(g * LANES, LANES), LANES)
        xs = xall[at].reshape(LANES, padded)
        gs = gall[at].reshape(LANES, dim)
        both = lax.dot_general(wgu[...], xs[:, :dim], (((1,), (1,)), ((), ())), preferred_element_type=F32)
        pre_gate, pre_up = both[:units], both[units:]
        back = lax.dot_general(wd[...], gs, (((1,), (1,)), ((), ())), preferred_element_type=F32)
        weight = lax.dot_general(
            own_lane, xs[:, dim:], (((1,), (1,)), ((), ())), preferred_element_type=F32
        )[0:1, :]
        sigmoid = 1.0 / (1.0 + jnp.exp(-pre_gate))
        silu = pre_gate * sigmoid
        active = silu * pre_up
        total = jnp.sum(active * back, axis=0, keepdims=True)
        total = jnp.transpose(jnp.broadcast_to(total, (LANES, LANES)))
        scaled_t[:, cols] = (weight * active).astype(BF16)
        weighted = weight * back
        d_gate = (weighted * pre_up * sigmoid * (1.0 + pre_gate * (1.0 - sigmoid))).astype(BF16)
        d_up = (weighted * silu).astype(BF16)
        dcat[:units, cols] = d_gate
        dcat[units:, cols] = d_up
        rows = lax.dot_general(
            dcat[:, cols], wgu[...], (((0,), (0,)), ((), ())), preferred_element_type=F32
        ).reshape(per, CAP, dim)
        rfull[at, :, :dim] = rows
        rhalf[at, :, :dim] = rows.astype(BF16)
        rfull[at, :, dim:] = total.reshape(per, CAP, LANES)
        rhalf[at, :, dim:] = split(total).reshape(per, CAP, LANES)
        return 0

    lax.fori_loop(0, 2 * nz // per, group, 0)

    crossing = []
    for d in range(nz):
        z = (mz + nz // 2 + d) % nz
        crossing.append(
            send(rhalf.at[2 * z + 1 - core], sib.at[z], ss.at[d], rs.at[d], sibling)
        )

    tile = min(512, dim)

    def weights(n, _):
        cols = pl.ds(pl.multiple_of(n * tile, tile), tile)
        flat = 2 * nz * CAP
        grads = jnp.dot(dcat[...], xall[:, :, cols].reshape(flat, tile), preferred_element_type=F32)
        out_gate[:, cols] = grads[:units]
        out_up[:, cols] = grads[units:]
        out_down[:, cols] = jnp.dot(
            scaled_t[...], gall[:, :, cols].reshape(flat, tile), preferred_element_type=F32
        )
        return 0

    lax.fori_loop(0, dim // tile, weights, 0)
    for copy in crossing:
        copy.wait_recv()

    def low_part(z):
        return rfull[2 * z + core, :, :half] + sib[z, :, :half].astype(F32)

    def high_part(z):
        return rfull[2 * z + core, :, half:dim] + sib[z, :, half:dim].astype(F32)

    def gate_part(z):
        return rfull[2 * z + core, :, dim:] + join(sib[z, :, dim:])

    last = {}
    for step in range(long):
        for side, sign in ((0, 1), (1, -1)):
            to = at_z(up_z if side == 0 else down_z)
            hops = long if side == 0 else short
            if step < hops:
                if step:
                    last["lo", side].wait_recv()
                z = (mz + sign * (hops - step) + nz) % nz
                value = low_part(z)
                if step:
                    value = value + ring_recv_lo[side, step - 1].astype(F32)
                ring_send_lo[side, step] = value.astype(BF16)
                last["lo", side] = send(
                    ring_send_lo.at[side, step], ring_recv_lo.at[side, step],
                    slo.at[side, step], rlo.at[side, step], to,
                )
            hops = short if side == 0 else long
            if step < hops:
                if step:
                    last["hi", side].wait_recv()
                z = (mz + sign * (hops - step) + nz) % nz
                value, gate_value = high_part(z), gate_part(z)
                if step:
                    value = value + ring_recv_hi[side, step - 1, :, :half].astype(F32)
                    gate_value = gate_value + join(ring_recv_hi[side, step - 1, :, half:])
                ring_send_hi[side, step, :, :half] = value.astype(BF16)
                ring_send_hi[side, step, :, half:] = split(gate_value)
                last["hi", side] = send(
                    ring_send_hi.at[side, step], ring_recv_hi.at[side, step],
                    shi.at[side, step], rhi.at[side, step], to,
                )

    def back_to_tokens(place, rows):
        return lax.dot_general(
            place.astype(BF16), rows, (((0,), (0,)), ((), ())), preferred_element_type=F32
        ).astype(BF16)

    low = low_part(mz)
    for side, hops in ((0, long), (1, short)):
        last["lo", side].wait_recv()
        low = low + ring_recv_lo[side, hops - 1].astype(F32)
    c1[...] = back_to_tokens(place_a, low.astype(BF16)).reshape(ny, 2 * nx, half)
    c_sends = []
    for d in range(1, ny):
        y = (my + d) % ny
        c_sends.append(send(c1.at[y], c1r.at[my], s3a.at[d], r3a.at[d], at_y(y)))
    c1r[my] = c1[my]

    high, gate_row = high_part(mz), gate_part(mz)
    for side, hops in ((0, short), (1, long)):
        last["hi", side].wait_recv()
        high = high + ring_recv_hi[side, hops - 1, :, :half].astype(F32)
        gate_row = gate_row + join(ring_recv_hi[side, hops - 1, :, half:])
    lanes = lax.broadcasted_iota(jnp.int32, (CAP, LANES), 1)
    gate_row = jnp.where(lanes % (LANES // 2) == mine, split(gate_row).astype(F32), 0.0).astype(BF16)
    e1[:, :, :half] = back_to_tokens(place_b, high.astype(BF16)).reshape(nx, 2 * ny, half)
    e1[:, :, half:] = back_to_tokens(place_b, gate_row).reshape(nx, 2 * ny, LANES)
    e_sends = []
    for d in range(1, nx):
        x = (mx + d) % nx
        e_sends.append(send(e1.at[x], e1r.at[mx], s3b.at[d], r3b.at[d], at_x(x)))
    e1r[mx] = e1[mx]

    def total_of(buf, count):
        value = buf[0].astype(F32)
        for k in range(1, count):
            value = value + buf[k].astype(F32)
        return value

    for copy in c_sends:
        copy.wait_recv()
    flat_a[:, :half] = total_of(c1r, ny)
    for k in range(nx):
        c2[k] = flat_a[2 * k : 2 * k + 2, :half]
    c_sends = []
    for d in range(1, nx):
        x = (mx + d) % nx
        c_sends.append(send(c2.at[x], c2r.at[mx], s4a.at[d], r4a.at[d], at_x(x)))
    c2r[mx] = c2[mx]

    for copy in e_sends:
        copy.wait_recv()
    flat_b[:, : half + LANES] = total_of(e1r, nx)
    for k in range(ny):
        e2[k] = flat_b[2 * k : 2 * k + 2, : half + LANES]
    e_sends = []
    for d in range(1, ny):
        y = (my + d) % ny
        e_sends.append(send(e2.at[y], e2r.at[my], s4b.at[d], r4b.at[d], at_y(y)))
    e2r[my] = e2[my]

    for copy in c_sends:
        copy.wait_recv()
    out_in[:, :half] = total_of(c2r, nx)
    for copy in e_sends:
        copy.wait_recv()
    final = total_of(e2r, ny)
    out_in[:, half:] = final[:, :half]
    out_gate_rows[...] = final[:, half:]
    for copy in pending:
        copy.wait_send()


def on_device(nx, ny, nz, tokens, grad_out, expert_ids, router_logits, w_gate, w_up, w_down):
    peers = nx * ny
    dim, units = w_gate.shape[1], w_gate.shape[2]
    padded, half = dim + LANES, dim // 2
    long = nz // 2
    raised = jnp.exp(router_logits[0])
    gate_probs = raised / jnp.sum(raised, axis=-1, keepdims=True)
    gate_rows = gate_probs.astype(BF16)
    chosen = expert_ids[0][:, :, None] == jnp.arange(LANES, dtype=jnp.int32)[None, None, :]
    table = jnp.sum(jnp.where(chosen, gate_rows.astype(F32)[:, :, None], 0.0), axis=1).astype(BF16)
    xin = jnp.concatenate([tokens[0], table], axis=1)
    gin = jnp.concatenate([grad_out[0], table], axis=1)
    wgu = jnp.concatenate([jnp.swapaxes(w_gate[0], 0, 1), jnp.swapaxes(w_up[0], 0, 1)], axis=0)
    vmem, dma = pltpu.VMEM, pltpu.SemaphoreType.DMA
    wide = half + LANES
    scratch = [
        vmem((nx, 2, padded), BF16), vmem((ny, 2, padded), BF16),
        vmem((2 * nx, padded), F32), vmem((2 * ny, padded), F32),
        vmem((ny, 2 * nx, padded), BF16), vmem((nx, 2 * ny, padded), BF16),
        vmem((2 * nz, CAP, padded), BF16), vmem((2 * nz, CAP, dim), BF16),
        vmem((2 * units, 2 * nz * CAP), BF16), vmem((units, 2 * nz * CAP), BF16),
        vmem((2 * nz, CAP, padded), F32), vmem((2 * nz, CAP, padded), BF16),
        vmem((nz, CAP, padded), BF16),
        vmem((2, long, CAP, half), BF16), vmem((2, long, CAP, half), BF16),
        vmem((2, long, CAP, wide), BF16), vmem((2, long, CAP, wide), BF16),
        vmem((ny, 2 * nx, half), BF16), vmem((ny, 2 * nx, half), BF16),
        vmem((nx, 2 * ny, wide), BF16), vmem((nx, 2 * ny, wide), BF16),
        vmem((nx, 2, half), F32), vmem((nx, 2, half), F32),
        vmem((ny, 2, wide), F32), vmem((ny, 2, wide), F32),
    ]
    for count in (nx, nx, ny, ny, ny, ny, nx, nx):
        scratch.append(dma((count,)))
    for _ in range(2):
        scratch += [dma((2, long)), dma((2, long)), dma((2 * long + 1,)), dma((2 * long + 1,))]
    scratch += [dma((nz,)), dma((nz,)), dma((2, long)), dma((2, long)), dma((2, long)), dma((2, long))]
    for count in (ny, ny, nx, nx, nx, nx, ny, ny):
        scratch.append(dma((count,)))
    spec = pl.BlockSpec(memory_space=pltpu.VMEM)
    rows, gate_dense, sum_gate, sum_up, sum_down = pl.pallas_call(
        functools.partial(kernel, nx, ny, nz),
        out_shape=[
            jax.ShapeDtypeStruct((2, dim), F32),
            jax.ShapeDtypeStruct((2, LANES), F32),
            jax.ShapeDtypeStruct((units, dim), F32),
            jax.ShapeDtypeStruct((units, dim), F32),
            jax.ShapeDtypeStruct((units, dim), F32),
        ],
        in_specs=[spec] * 4,
        out_specs=[spec] * 5,
        scratch_shapes=scratch,
        compiler_params=pltpu.CompilerParams(
            collective_id=0, has_side_effects=True, vmem_limit_bytes=56 * 1024 * 1024
        ),
    )(xin, gin, wgu, w_down[0])
    per_expert = gate_dense[:, : LANES // 2] + gate_dense[:, LANES // 2 :]
    gate_grad = jnp.sum(
        jnp.where(chosen[:, :, : LANES // 2], per_expert[:, None, :], 0.0), axis=-1
    )
    grad_logits = gate_probs * (gate_grad - jnp.sum(gate_probs * gate_grad, axis=-1, keepdims=True))
    return (
        rows[None],
        grad_logits[None],
        jnp.swapaxes(sum_gate, 0, 1)[None],
        jnp.swapaxes(sum_up, 0, 1)[None],
        sum_down[None],
    )


def solution(mesh):
    side = math.isqrt(mesh.shape["expert"])
    nz = mesh.shape["hidden"] // 2
    token_spec, wide, tall = P("hidden", "expert", None), P("expert", None, "hidden"), P("expert", "hidden", None)
    return jax.shard_map(
        functools.partial(on_device, side, side, nz),
        mesh=mesh,
        in_specs=(token_spec,) * 4 + (wide, wide, tall),
        out_specs=(token_spec, token_spec, wide, wide, tall),
        check_vma=False,
    )
```

```python
import functools
import math

import jax
import jax.numpy as jnp
from jax import lax
from jax.experimental import pallas as pl
from jax.experimental.pallas import tpu as pltpu
from jax.sharding import PartitionSpec as P

MESH = pl.DeviceIdType.MESH
CAP = 32
LANES = 128
F32 = jnp.float32
BF16 = jnp.bfloat16
TRANSPOSED_RIGHT = (((1,), (1,)), ((), ()))
TRANSPOSED_LEFT = (((0,), (0,)), ((), ()))


def split(value):
    lane = lax.broadcasted_iota(jnp.int32, value.shape, value.ndim - 1)
    high = value.astype(BF16).astype(F32)
    return jnp.where(lane < LANES // 2, high, value - high).astype(BF16)


def join(parts):
    wide = parts.astype(F32)
    return wide + pltpu.roll(wide, LANES // 2, 1)


def sections_of(dim):
    half, quarter = dim // 2, dim // 4
    return [
        (True, 0, quarter, False),
        (False, half, quarter, True),
        (True, quarter, quarter, False),
        (False, half + quarter, quarter, False),
    ]


def scratch_of(nx, ny, nz, dim, units):
    vmem, dma = pltpu.VMEM, pltpu.SemaphoreType.DMA
    half, padded, long = dim // 2, dim + LANES, nz // 2
    wide = half + LANES
    flat = 2 * nz * CAP
    shapes = {
        "xa": vmem((2, wide), BF16), "xb": vmem((2, wide), BF16),
        "xa1": vmem((nx, 2, wide), BF16), "xb1": vmem((ny, 2, wide), BF16),
        "ga1": vmem((nx, 2, half), BF16), "gb1": vmem((ny, 2, half), BF16),
        "flat_a": vmem((2 * nx, wide), F32), "flat_b": vmem((2 * ny, wide), F32),
        "xa2": vmem((ny, 2 * nx, wide), BF16), "xb2": vmem((nx, 2 * ny, wide), BF16),
        "ga2": vmem((ny, 2 * nx, half), BF16), "gb2": vmem((nx, 2 * ny, half), BF16),
        "xlo": vmem((2 * nz, CAP, half), BF16), "xhi": vmem((2 * nz, CAP, wide), BF16),
        "glo": vmem((2 * nz, CAP, half), BF16), "ghi": vmem((2 * nz, CAP, half), BF16),
        "wgu": vmem((2 * units, dim), BF16), "wd": vmem((units, dim), BF16),
        "pre": vmem((2 * units, flat), F32), "weight": vmem((8, flat), F32),
        "dcat": vmem((2 * units, flat), BF16), "scaled": vmem((units, flat), BF16),
        "rfull": vmem((2 * nz, CAP, padded), F32), "rhalf": vmem((2 * nz, CAP, padded), BF16),
        "sib": vmem((nz, CAP, padded), BF16),
        "sums": vmem((2 * units, dim), F32), "sums_down": vmem((units, dim), F32),
        "ssem": dma((256,)), "rsem": dma((256,)), "lsem": dma((8,)),
    }
    for n, (first_y, _, width, gate) in enumerate(sections_of(dim)):
        size = width + (LANES if gate else 0)
        one, two = (ny, nx) if first_y else (nx, ny)
        shapes[f"put{n}"] = vmem((2, long, CAP, size), BF16)
        shapes[f"got{n}"] = vmem((2, long, CAP, size), BF16)
        shapes[f"c{n}"] = vmem((one, 2 * two, size), BF16)
        shapes[f"cr{n}"] = vmem((one, 2 * two, size), BF16)
        shapes[f"e{n}"] = vmem((two, 2, size), F32)
        shapes[f"er{n}"] = vmem((two, 2, size), F32)
        shapes[f"flat{n}"] = vmem((2 * two, size), F32)
    return shapes


def kernel(
    nx, ny, nz, names,
    tok, grd, ids, logits, wg, wu, wdn,
    out_in, out_logits, out_gate, out_up, out_down, *scratch,
):
    s = dict(zip(names, scratch))
    mine = lax.axis_index("expert")
    hid = lax.axis_index("hidden")
    mx, my = mine // ny, mine % ny
    mz, core = hid // 2, hid % 2
    units, dim = wdn.shape
    top = ids.shape[1]
    half = dim // 2
    tokens = 2 * nx * ny
    long, short = nz // 2, nz // 2 - 1

    def at_x(x):
        return {"expert": x * ny + my, "hidden": hid}

    def at_y(y):
        return {"expert": mx * ny + y, "hidden": hid}

    def at_z(z):
        return {"expert": mine, "hidden": 2 * z + core}

    sibling = {"expert": mine, "hidden": 2 * mz + 1 - core}
    up_z, down_z = (mz + 1) % nz, (mz + nz - 1) % nz
    pending = []

    def send(src, dst, device):
        number = len(pending)
        copy = pltpu.make_async_remote_copy(
            src_ref=src, dst_ref=dst, send_sem=s["ssem"].at[number], recv_sem=s["rsem"].at[number],
            device_id=device, device_id_type=MESH,
        )
        copy.start()
        pending.append(copy)
        return copy

    def arrive(copies):
        for copy in copies:
            copy.wait_recv()

    barrier = pltpu.get_barrier_semaphore()
    greet = [at_x((mx + d) % nx) for d in range(1, nx)]
    greet += [at_y((my + d) % ny) for d in range(1, ny)]
    greet += [at_z(up_z), at_z(down_z), sibling]
    for device in greet:
        pl.semaphore_signal(barrier, inc=1, device_id=device, device_id_type=MESH)

    loads = [
        pltpu.make_async_copy(wg, s["wgu"].at[pl.ds(0, units)], s["lsem"].at[0]),
        pltpu.make_async_copy(wu, s["wgu"].at[pl.ds(units, units)], s["lsem"].at[1]),
        pltpu.make_async_copy(wdn, s["wd"], s["lsem"].at[2]),
    ]
    for load in loads:
        load.start()

    raised = jnp.exp(logits[...])
    probs = raised / jnp.sum(raised, axis=-1, keepdims=True)
    lane_of = lax.broadcasted_iota(jnp.int32, (2, LANES), 1)
    hits = [lane_of == ids[:, k : k + 1] for k in range(top)]
    spread = jnp.zeros((2, LANES), F32)
    for k in range(top):
        spread = spread + jnp.where(hits[k], probs[:, k : k + 1], 0.0)
    table = spread.astype(BF16)
    s["xa"][:, :half] = tok[:, :half]
    s["xb"][:, :half] = tok[:, half:]
    s["xa"][:, half:] = table
    s["xb"][:, half:] = table
    pl.semaphore_wait(barrier, len(greet))

    def spread_x(src, dst):
        return [send(src, dst.at[mx], at_x((mx + d) % nx)) for d in range(1, nx)]

    def spread_y(src, dst):
        return [send(src, dst.at[my], at_y((my + d) % ny)) for d in range(1, ny)]

    xa = spread_x(s["xa"], s["xa1"])
    xb = spread_y(s["xb"], s["xb1"])
    s["xa1"][mx] = s["xa"][...]
    s["xb1"][my] = s["xb"][...]
    ga = spread_x(grd.at[:, pl.ds(0, half)], s["ga1"])
    gb = spread_y(grd.at[:, pl.ds(half, half)], s["gb1"])
    s["ga1"][mx] = grd[:, :half]
    s["gb1"][my] = grd[:, half:]

    def flatten(blocks, wide):
        count, _, width = blocks.shape
        for k in range(count):
            wide[2 * k : 2 * k + 2, :width] = blocks[k].astype(F32)
        return wide[:, :width].astype(BF16)

    arrive(xa)
    s["xa2"][my] = flatten(s["xa1"], s["flat_a"])
    xa = spread_y(s["xa2"].at[my], s["xa2"])
    arrive(xb)
    s["xb2"][mx] = flatten(s["xb1"], s["flat_b"])
    xb = spread_x(s["xb2"].at[mx], s["xb2"])
    arrive(ga)
    s["ga2"][my] = flatten(s["ga1"], s["flat_a"])
    ga = spread_y(s["ga2"].at[my], s["ga2"])
    arrive(gb)
    s["gb2"][mx] = flatten(s["gb1"], s["flat_b"])
    gb = spread_x(s["gb2"].at[mx], s["gb2"])

    own_lane = jnp.where(lax.broadcasted_iota(jnp.int32, (8, LANES), 1) == mine, 1.0, 0.0).astype(BF16)

    def order_a(t):
        return t

    def order_b(t):
        xx, yy, jj = t // (2 * ny), (t // 2) % ny, t % 2
        return (yy * nx + xx) * 2 + jj

    def placing_of(gates, order):
        gate = lax.dot_general(own_lane, gates, TRANSPOSED_RIGHT, preferred_element_type=F32)
        picked = jnp.where(gate > 0.0, 1.0, 0.0)
        before = order(lax.broadcasted_iota(jnp.int32, (tokens, tokens), 0))
        after = order(lax.broadcasted_iota(jnp.int32, (tokens, tokens), 1))
        upto = jnp.where(before <= after, 1.0, 0.0).astype(BF16)
        rank = jnp.dot(picked.astype(BF16), upto, preferred_element_type=F32) - 1.0
        rank = jnp.where(picked > 0.0, rank, -1.0)
        slot = lax.broadcasted_iota(jnp.int32, (CAP, tokens), 0).astype(F32)
        return jnp.where(rank[0:1, :] == slot, 1.0, 0.0).astype(BF16)

    def ring_start(buf, hops):
        own = buf.at[hid]
        waits = [send(own, own, at_z(up_z)), send(own, own, at_z(down_z))]
        return buf, hops, waits, [send(own, own, sibling)]

    def ring_step(ring, step):
        buf, hops, waits, over = ring
        for side, sign in ((0, 1), (1, -1)) if hops[0] >= hops[1] else ((1, -1), (0, 1)):
            if step >= hops[side]:
                continue
            waits[side].wait_recv()
            block = buf.at[2 * ((mz - sign * (step + 1) + nz) % nz) + core]
            if step + 1 < hops[side]:
                waits[side] = send(block, block, at_z(up_z if side == 0 else down_z))
            over.append(send(block, block, sibling))

    arrive(xa)
    wide_a = s["xa2"][...].reshape(tokens, half + LANES)
    place_a = placing_of(wide_a[:, half:], order_a)
    s["xlo"][hid] = jnp.dot(place_a, wide_a[:, :half], preferred_element_type=F32).astype(BF16)
    x_low = ring_start(s["xlo"], (long, short))
    arrive(xb)
    wide_b = s["xb2"][...].reshape(tokens, half + LANES)
    place_b = placing_of(wide_b[:, half:], order_b)
    s["xhi"][hid] = jnp.dot(place_b, wide_b, preferred_element_type=F32).astype(BF16)
    x_high = ring_start(s["xhi"], (short, long))
    ring_step(x_low, 0)
    ring_step(x_high, 0)
    arrive(ga)
    s["glo"][hid] = jnp.dot(
        place_a, s["ga2"][...].reshape(tokens, half), preferred_element_type=F32
    ).astype(BF16)
    g_low = ring_start(s["glo"], (long, short))
    arrive(gb)
    s["ghi"][hid] = jnp.dot(
        place_b, s["gb2"][...].reshape(tokens, half), preferred_element_type=F32
    ).astype(BF16)
    g_high = ring_start(s["ghi"], (short, long))
    for step in range(1, long):
        ring_step(x_low, step)
        ring_step(x_high, step)
        ring_step(g_low, step - 1)
        ring_step(g_high, step - 1)
    arrive(x_low[3] + x_high[3])

    def z_at(p):
        step = (p + 1) // 2
        return (mz + nz // 2 + (1 - 2 * (p % 2)) * step + nz) % nz

    def rows_at(buf, p, columns):
        return buf[pl.ds(2 * z_at(p), 2), :, columns].reshape(2 * CAP, -1)

    pair = LANES // (2 * CAP)

    def rows_of(buf, g, columns):
        return jnp.concatenate([rows_at(buf, g * pair + i, columns) for i in range(pair)], axis=0)

    for load in loads:
        load.wait()
    every, low, high = slice(None), slice(0, half), slice(half, dim)

    def forward(g, _):
        cols = pl.ds(pl.multiple_of(g * LANES, LANES), LANES)
        x_hi = rows_of(s["xhi"], g, every)
        s["pre"][:, cols] = lax.dot_general(
            s["wgu"][:, low], rows_of(s["xlo"], g, every), TRANSPOSED_RIGHT, preferred_element_type=F32
        ) + lax.dot_general(
            s["wgu"][:, high], x_hi[:, :half], TRANSPOSED_RIGHT, preferred_element_type=F32
        )
        s["weight"][:, cols] = lax.dot_general(
            own_lane, x_hi[:, half:], TRANSPOSED_RIGHT, preferred_element_type=F32
        )
        return 0

    groups = nz // pair
    lax.fori_loop(0, groups, forward, 0)
    ring_step(g_low, long - 1)
    ring_step(g_high, long - 1)
    arrive(g_low[3] + g_high[3])

    crossing = []
    for g in range(groups):
        cols = slice(g * LANES, (g + 1) * LANES)
        back = lax.dot_general(
            s["wd"][:, low], rows_of(s["glo"], g, every), TRANSPOSED_RIGHT, preferred_element_type=F32
        ) + lax.dot_general(
            s["wd"][:, high], rows_of(s["ghi"], g, every), TRANSPOSED_RIGHT, preferred_element_type=F32
        )
        pre_gate, pre_up = s["pre"][:units, cols], s["pre"][units:, cols]
        weight = s["weight"][0:1, cols]
        sigmoid = 1.0 / (1.0 + jnp.exp(-pre_gate))
        silu = pre_gate * sigmoid
        active = silu * pre_up
        total = jnp.sum(active * back, axis=0, keepdims=True)
        total = jnp.transpose(jnp.broadcast_to(total, (LANES, LANES)))
        s["scaled"][:, cols] = (weight * active).astype(BF16)
        weighted = weight * back
        s["dcat"][:units, cols] = (
            weighted * pre_up * sigmoid * (1.0 + pre_gate * (1.0 - sigmoid))
        ).astype(BF16)
        s["dcat"][units:, cols] = (weighted * silu).astype(BF16)
        rows = lax.dot_general(
            s["dcat"][:, cols], s["wgu"][...], TRANSPOSED_LEFT, preferred_element_type=F32
        )
        for i in range(pair):
            z = z_at(g * pair + i)
            part = slice(2 * CAP * i, 2 * CAP * (i + 1))
            at = pl.ds(2 * z, 2)
            mine_rows, mine_total = rows[part].reshape(2, CAP, dim), total[part].reshape(2, CAP, LANES)
            s["rfull"][at, :, :dim] = mine_rows
            s["rhalf"][at, :, :dim] = mine_rows.astype(BF16)
            s["rfull"][at, :, dim:] = mine_total
            s["rhalf"][at, :, dim:] = split(mine_total)
            crossing.append(send(s["rhalf"].at[2 * z + 1 - core], s["sib"].at[z], sibling))

    tile = dim // 4

    def weights(n):
        cols = slice(n * tile, (n + 1) * tile)
        at = slice(n % 2 * tile, n % 2 * tile + tile)
        x_rows = jnp.concatenate([rows_at(s["xlo" if n < 2 else "xhi"], p, at) for p in range(nz)], axis=0)
        s["sums"][:, cols] = jnp.dot(s["dcat"][...], x_rows, preferred_element_type=F32)
        g_rows = jnp.concatenate([rows_at(s["glo" if n < 2 else "ghi"], p, at) for p in range(nz)], axis=0)
        s["sums_down"][:, cols] = jnp.dot(s["scaled"][...], g_rows, preferred_element_type=F32)

    sections = sections_of(dim)

    def piece(section, z):
        _, start, width, gate = section
        cols = slice(start, start + width)
        value = s["rfull"][2 * z + core, :, cols] + s["sib"][z, :, cols].astype(F32)
        if not gate:
            return value, None
        return value, s["rfull"][2 * z + core, :, dim:] + join(s["sib"][z, :, dim:])

    def add(value, ref, width):
        rows, gate_rows = value
        rows = rows + ref[:, :width].astype(F32)
        if gate_rows is not None:
            gate_rows = gate_rows + join(ref[:, width:])
        return rows, gate_rows

    crossed = set()

    def need(p):
        if p not in crossed:
            crossing[p].wait_recv()
            crossed.add(p)

    def place_of(distance):
        far = distance % nz - nz // 2
        return 2 * far if far >= 0 else -2 * far - 1

    last = {}
    for step in range(long):
        for n, section in enumerate(sections):
            hops = (long, short) if section[0] else (short, long)
            width = section[2]
            for side, sign in ((0, 1), (1, -1)):
                if step >= hops[side]:
                    continue
                if step:
                    last[n, side].wait_recv()
                distance = sign * (hops[side] - step)
                need(place_of(distance))
                value = piece(section, (mz + distance + nz) % nz)
                if step:
                    value = add(value, s[f"got{n}"].at[side, step - 1], width)
                put = s[f"put{n}"].at[side, step]
                put[:, :width] = value[0].astype(BF16)
                if section[3]:
                    put[:, width:] = split(value[1])
                last[n, side] = send(
                    put, s[f"got{n}"].at[side, step], at_z(up_z if side == 0 else down_z)
                )
        if step == 0:
            weights(0)
            weights(1)
        elif step < 3:
            weights(step + 1)
    for n in range(min(long, 3) + 1, 4):
        weights(n)
    stores = [
        pltpu.make_async_copy(s["sums"].at[pl.ds(0, units)], out_gate, s["lsem"].at[3]),
        pltpu.make_async_copy(s["sums"].at[pl.ds(units, units)], out_up, s["lsem"].at[4]),
        pltpu.make_async_copy(s["sums_down"], out_down, s["lsem"].at[5]),
    ]
    for store in stores:
        store.start()

    def back_to_tokens(place, rows):
        return lax.dot_general(place, rows, TRANSPOSED_LEFT, preferred_element_type=F32).astype(BF16)

    need(place_of(0))
    first, second = [], []
    for n, section in enumerate(sections):
        first_y, start, width, gate = section
        value = piece(section, mz)
        for side, hops in enumerate((long, short) if first_y else (short, long)):
            last[n, side].wait_recv()
            value = add(value, s[f"got{n}"].at[side, hops - 1], width)
        c, cr = s[f"c{n}"], s[f"cr{n}"]
        place = place_a if first_y else place_b
        c[:, :, :width] = back_to_tokens(place, value[0].astype(BF16)).reshape(c.shape[0], c.shape[1], width)
        if gate:
            lanes = lax.broadcasted_iota(jnp.int32, (CAP, LANES), 1)
            here = jnp.where(lanes % (LANES // 2) == mine, split(value[1]).astype(F32), 0.0).astype(BF16)
            c[:, :, width:] = back_to_tokens(place, here).reshape(c.shape[0], c.shape[1], LANES)
        if first_y:
            peers = [(my + d) % ny for d in range(1, ny)]
            first.append([send(c.at[y], cr.at[my], at_y(y)) for y in peers])
            cr[my] = c[my]
        else:
            peers = [(mx + d) % nx for d in range(1, nx)]
            first.append([send(c.at[x], cr.at[mx], at_x(x)) for x in peers])
            cr[mx] = c[mx]

    def total_of(buf):
        value = buf[0].astype(F32)
        for k in range(1, buf.shape[0]):
            value = value + buf[k].astype(F32)
        return value

    for n, section in enumerate(sections):
        arrive(first[n])
        e, er, wide = s[f"e{n}"], s[f"er{n}"], s[f"flat{n}"]
        wide[...] = total_of(s[f"cr{n}"])
        for k in range(e.shape[0]):
            e[k] = wide[2 * k : 2 * k + 2, :]
        if section[0]:
            peers = [(mx + d) % nx for d in range(1, nx)]
            second.append([send(e.at[x], er.at[mx], at_x(x)) for x in peers])
            er[mx] = e[mx]
        else:
            peers = [(my + d) % ny for d in range(1, ny)]
            second.append([send(e.at[y], er.at[my], at_y(y)) for y in peers])
            er[my] = e[my]

    for n, (_, start, width, gate) in enumerate(sections):
        arrive(second[n])
        final = total_of(s[f"er{n}"])
        out_in[:, start : start + width] = final[:, :width]
        if gate:
            grads = join(final[:, width:])
            inner = jnp.sum(spread * grads, axis=-1, keepdims=True)
            place = lax.broadcasted_iota(jnp.int32, (2, top), 1)
            result = jnp.zeros((2, top), F32)
            for k in range(top):
                own = jnp.sum(jnp.where(hits[k], grads, 0.0), axis=-1, keepdims=True)
                result = result + jnp.where(place == k, probs[:, k : k + 1] * (own - inner), 0.0)
            out_logits[...] = result
    for store in stores:
        store.wait()
    for copy in pending:
        copy.wait_send()


def hand_over(*refs):
    count = len(refs) // 2
    sources, results, sem = refs[:count], refs[count : 2 * count], refs[-1]
    copies = []
    for source, result in zip(sources, results):
        rows = source.shape[0]
        cuts = 3 if rows % 24 == 0 else 1
        for k in range(cuts):
            at = pl.ds(k * (rows // cuts), rows // cuts)
            copies.append(pltpu.make_async_copy(source.at[at], result.at[at], sem.at[len(copies)]))
    for copy in copies:
        copy.start()
    for copy in copies:
        copy.wait()


def on_device(nx, ny, nz, tokens, grad_out, expert_ids, router_logits, w_gate, w_up, w_down):
    dim, units = w_gate.shape[1], w_gate.shape[2]
    shapes = scratch_of(nx, ny, nz, dim, units)
    spec = pl.BlockSpec(memory_space=pltpu.VMEM)
    anywhere = pl.BlockSpec(memory_space=pl.ANY)
    out_shape = [
        jax.ShapeDtypeStruct((2, dim), F32),
        jax.ShapeDtypeStruct(expert_ids.shape[1:], F32),
        jax.ShapeDtypeStruct((units, dim), F32),
        jax.ShapeDtypeStruct((units, dim), F32),
        jax.ShapeDtypeStruct((units, dim), F32),
    ]
    results = pl.pallas_call(
        functools.partial(kernel, nx, ny, nz, tuple(shapes)),
        out_shape=out_shape,
        in_specs=[spec] * 4 + [anywhere] * 3,
        out_specs=[spec] * 2 + [anywhere] * 3,
        scratch_shapes=list(shapes.values()),
        compiler_params=pltpu.CompilerParams(
            collective_id=0, has_side_effects=True, vmem_limit_bytes=56 * 1024 * 1024
        ),
    )(
        tokens[0], grad_out[0], expert_ids[0], router_logits[0],
        jnp.swapaxes(w_gate[0], 0, 1), jnp.swapaxes(w_up[0], 0, 1), w_down[0],
    )
    rows, logit_grads, sum_gate, sum_up, sum_down = pl.pallas_call(
        hand_over,
        out_shape=out_shape,
        in_specs=[anywhere] * 5,
        out_specs=[anywhere] * 5,
        scratch_shapes=[pltpu.SemaphoreType.DMA((11,))],
    )(*results)
    return (
        rows[None],
        logit_grads[None],
        jnp.swapaxes(sum_gate, 0, 1)[None],
        jnp.swapaxes(sum_up, 0, 1)[None],
        sum_down[None],
    )


def solution(mesh):
    side = math.isqrt(mesh.shape["expert"])
    nz = mesh.shape["hidden"] // 2
    token_spec, wide, tall = P("hidden", "expert", None), P("expert", None, "hidden"), P("expert", "hidden", None)
    return jax.shard_map(
        functools.partial(on_device, side, side, nz),
        mesh=mesh,
        in_specs=(token_spec,) * 4 + (wide, wide, tall),
        out_specs=(token_spec, token_spec, wide, wide, tall),
        check_vma=False,
    )
```

```python
import functools
import math

import jax
import jax.numpy as jnp
from jax import lax
from jax.experimental import pallas as pl
from jax.experimental.pallas import tpu as pltpu
from jax.sharding import PartitionSpec as P

MESH = pl.DeviceIdType.MESH
CAP = 32
LANES = 128
F32 = jnp.float32
BF16 = jnp.bfloat16
TRANSPOSED_RIGHT = (((1,), (1,)), ((), ()))
TRANSPOSED_LEFT = (((0,), (0,)), ((), ()))


def split(value):
    lane = lax.broadcasted_iota(jnp.int32, value.shape, value.ndim - 1)
    high = value.astype(BF16).astype(F32)
    return jnp.where(lane < LANES // 2, high, value - high).astype(BF16)


def join(parts):
    wide = parts.astype(F32)
    return wide + pltpu.roll(wide, LANES // 2, 1)


def sections_of(dim):
    half, quarter = dim // 2, dim // 4
    return [
        (True, 0, quarter, False),
        (False, half, quarter, True),
        (True, quarter, quarter, False),
        (False, half + quarter, quarter, False),
    ]


def scratch_of(nx, ny, nz, dim, units):
    vmem, dma = pltpu.VMEM, pltpu.SemaphoreType.DMA
    half, padded, long = dim // 2, dim + LANES, nz // 2
    wide = half + LANES
    flat = 2 * nz * CAP
    shapes = {
        "xa": vmem((2, wide), BF16), "xb": vmem((2, wide), BF16),
        "xa1": vmem((nx, 2, wide), BF16), "xb1": vmem((ny, 2, wide), BF16),
        "ga1": vmem((nx, 2, half), BF16), "gb1": vmem((ny, 2, half), BF16),
        "flat_a": vmem((2 * nx, wide), F32), "flat_b": vmem((2 * ny, wide), F32),
        "xa2": vmem((ny, 2 * nx, wide), BF16), "xb2": vmem((nx, 2 * ny, wide), BF16),
        "ga2": vmem((ny, 2 * nx, half), BF16), "gb2": vmem((nx, 2 * ny, half), BF16),
        "xlo": vmem((2 * nz, CAP, half), BF16), "xhi": vmem((2 * nz, CAP, wide), BF16),
        "glo": vmem((2 * nz, CAP, half), BF16), "ghi": vmem((2 * nz, CAP, half), BF16),
        "wgu": vmem((2 * units, dim), BF16), "wd": vmem((units, dim), BF16),
        "pre": vmem((2 * units, flat), F32), "weight": vmem((8, flat), F32),
        "dcat": vmem((2 * units, flat), BF16), "scaled": vmem((units, flat), BF16),
        "rfull": vmem((2 * nz, CAP, padded), F32), "rhalf": vmem((2 * nz, CAP, padded), BF16),
        "sib": vmem((nz, CAP, padded), BF16),
        "sums": vmem((2 * units, dim), F32), "sums_down": vmem((units, dim), F32),
        "ssem": dma((256,)), "rsem": dma((256,)), "lsem": dma((8,)),
    }
    for n, (first_y, _, width, gate) in enumerate(sections_of(dim)):
        size = width + (LANES if gate else 0)
        one, two = (ny, nx) if first_y else (nx, ny)
        shapes[f"put{n}"] = vmem((2, long, CAP, size), BF16)
        shapes[f"got{n}"] = vmem((2, long, CAP, size), BF16)
        shapes[f"c{n}"] = vmem((one, 2 * two, size), BF16)
        shapes[f"cr{n}"] = vmem((one, 2 * two, size), BF16)
        shapes[f"e{n}"] = vmem((two, 2, size), F32)
        shapes[f"er{n}"] = vmem((two, 2, size), F32)
        shapes[f"flat{n}"] = vmem((2 * two, size), F32)
    return shapes


def kernel(
    nx, ny, nz, names,
    tok, grd, ids, logits, wg, wu, wdn,
    out_in, out_logits, out_gate, out_up, out_down, *scratch,
):
    s = dict(zip(names, scratch))
    mine = lax.axis_index("expert")
    hid = lax.axis_index("hidden")
    mx, my = mine // ny, mine % ny
    mz, core = hid // 2, hid % 2
    units, dim = wdn.shape
    top = ids.shape[1]
    half = dim // 2
    tokens = 2 * nx * ny
    long, short = nz // 2, nz // 2 - 1

    def at_x(x):
        return {"expert": x * ny + my, "hidden": hid}

    def at_y(y):
        return {"expert": mx * ny + y, "hidden": hid}

    def at_z(z):
        return {"expert": mine, "hidden": 2 * z + core}

    sibling = {"expert": mine, "hidden": 2 * mz + 1 - core}
    up_z, down_z = (mz + 1) % nz, (mz + nz - 1) % nz
    pending = []

    def send(src, dst, device):
        number = len(pending)
        copy = pltpu.make_async_remote_copy(
            src_ref=src, dst_ref=dst, send_sem=s["ssem"].at[number], recv_sem=s["rsem"].at[number],
            device_id=device, device_id_type=MESH,
        )
        copy.start()
        pending.append(copy)
        return copy

    def arrive(copies):
        for copy in copies:
            copy.wait_recv()

    barrier = pltpu.get_barrier_semaphore()
    greet = [at_x((mx + d) % nx) for d in range(1, nx)]
    greet += [at_y((my + d) % ny) for d in range(1, ny)]
    greet += [at_z(up_z), at_z(down_z), sibling]
    for device in greet:
        pl.semaphore_signal(barrier, inc=1, device_id=device, device_id_type=MESH)

    loads = [
        pltpu.make_async_copy(wg, s["wgu"].at[pl.ds(0, units)], s["lsem"].at[0]),
        pltpu.make_async_copy(wu, s["wgu"].at[pl.ds(units, units)], s["lsem"].at[1]),
        pltpu.make_async_copy(wdn, s["wd"], s["lsem"].at[2]),
    ]
    for load in loads:
        load.start()

    raised = jnp.exp(logits[...])
    probs = raised / jnp.sum(raised, axis=-1, keepdims=True)
    lane_of = lax.broadcasted_iota(jnp.int32, (2, LANES), 1)
    hits = [lane_of == ids[:, k : k + 1] for k in range(top)]
    spread = jnp.zeros((2, LANES), F32)
    for k in range(top):
        spread = spread + jnp.where(hits[k], probs[:, k : k + 1], 0.0)
    table = spread.astype(BF16)
    s["xa"][:, :half] = tok[:, :half]
    s["xb"][:, :half] = tok[:, half:]
    s["xa"][:, half:] = table
    s["xb"][:, half:] = table
    pl.semaphore_wait(barrier, len(greet))

    def spread_x(src, dst):
        return [send(src, dst.at[mx], at_x((mx + d) % nx)) for d in range(1, nx)]

    def spread_y(src, dst):
        return [send(src, dst.at[my], at_y((my + d) % ny)) for d in range(1, ny)]

    xa = spread_x(s["xa"], s["xa1"])
    xb = spread_y(s["xb"], s["xb1"])
    s["xa1"][mx] = s["xa"][...]
    s["xb1"][my] = s["xb"][...]
    ga = spread_x(grd.at[:, pl.ds(0, half)], s["ga1"])
    gb = spread_y(grd.at[:, pl.ds(half, half)], s["gb1"])
    s["ga1"][mx] = grd[:, :half]
    s["gb1"][my] = grd[:, half:]

    def flatten(blocks, wide):
        count, _, width = blocks.shape
        for k in range(count):
            wide[2 * k : 2 * k + 2, :width] = blocks[k].astype(F32)
        return wide[:, :width].astype(BF16)

    def ring_start(buf, at, place, size, hops, up, down, across):
        own = buf.at[at(place)]
        waits = [send(own, own, device) if hop else None for hop, device in zip(hops, (up, down))]
        over = {0: send(own, own, sibling)} if across else {}
        return buf, at, place, size, hops, (up, down), waits, over, across

    def ring_step(ring, step):
        buf, at, place, size, hops, devices, waits, over, across = ring
        for side in (0, 1) if hops[0] >= hops[1] else (1, 0):
            if step >= hops[side]:
                continue
            distance = -(step + 1) if side == 0 else step + 1
            waits[side].wait_recv()
            block = buf.at[at((place + distance + size) % size)]
            if step + 1 < hops[side]:
                waits[side] = send(block, block, devices[side])
            if across:
                over[distance % size] = send(block, block, sibling)

    def ring_x(buf, hops):
        return ring_start(buf, lambda x: x, mx, nx, hops, at_x((mx + 1) % nx), at_x((mx + nx - 1) % nx), False)

    def ring_y(buf, hops):
        return ring_start(buf, lambda y: y, my, ny, hops, at_y((my + 1) % ny), at_y((my + ny - 1) % ny), False)

    def ring_z(buf, hops):
        return ring_start(buf, lambda z: 2 * z + core, mz, nz, hops, at_z(up_z), at_z(down_z), True)

    def ways(size):
        return size // 2, size - 1 - size // 2

    arrive(xa)
    s["xa2"][my] = flatten(s["xa1"], s["flat_a"])
    xa = ring_y(s["xa2"], ways(ny))
    arrive(xb)
    s["xb2"][mx] = flatten(s["xb1"], s["flat_b"])
    xb = ring_x(s["xb2"], ways(nx))
    arrive(ga)
    s["ga2"][my] = flatten(s["ga1"], s["flat_a"])
    ga = ring_y(s["ga2"], ways(ny)[::-1])
    arrive(gb)
    s["gb2"][mx] = flatten(s["gb1"], s["flat_b"])
    gb = ring_x(s["gb2"], ways(nx)[::-1])
    last_step = max(nx, ny) // 2 - 1
    for step in range(last_step):
        for ring in (xa, xb, ga, gb):
            ring_step(ring, step)

    own_lane = jnp.where(lax.broadcasted_iota(jnp.int32, (8, LANES), 1) == mine, 1.0, 0.0).astype(BF16)

    def order_a(t):
        return t

    def order_b(t):
        xx, yy, jj = t // (2 * ny), (t // 2) % ny, t % 2
        return (yy * nx + xx) * 2 + jj

    def placing_of(gates, order):
        gate = lax.dot_general(own_lane, gates, TRANSPOSED_RIGHT, preferred_element_type=F32)
        picked = jnp.where(gate > 0.0, 1.0, 0.0)
        before = order(lax.broadcasted_iota(jnp.int32, (tokens, tokens), 0))
        after = order(lax.broadcasted_iota(jnp.int32, (tokens, tokens), 1))
        upto = jnp.where(before <= after, 1.0, 0.0).astype(BF16)
        rank = jnp.dot(picked.astype(BF16), upto, preferred_element_type=F32) - 1.0
        rank = jnp.where(picked > 0.0, rank, -1.0)
        slot = lax.broadcasted_iota(jnp.int32, (CAP, tokens), 0).astype(F32)
        return jnp.where(rank[0:1, :] == slot, 1.0, 0.0).astype(BF16)

    ring_step(xa, last_step)
    wide_a = s["xa2"][...].reshape(tokens, half + LANES)
    place_a = placing_of(wide_a[:, half:], order_a)
    s["xlo"][hid] = jnp.dot(place_a, wide_a[:, :half], preferred_element_type=F32).astype(BF16)
    x_low = ring_z(s["xlo"], (long, short))
    ring_step(xb, last_step)
    wide_b = s["xb2"][...].reshape(tokens, half + LANES)
    place_b = placing_of(wide_b[:, half:], order_b)
    s["xhi"][hid] = jnp.dot(place_b, wide_b, preferred_element_type=F32).astype(BF16)
    x_high = ring_z(s["xhi"], (short, long))
    ring_step(ga, last_step)
    s["glo"][hid] = jnp.dot(
        place_a, s["ga2"][...].reshape(tokens, half), preferred_element_type=F32
    ).astype(BF16)
    g_low = ring_z(s["glo"], (long, short))
    ring_step(gb, last_step)
    s["ghi"][hid] = jnp.dot(
        place_b, s["gb2"][...].reshape(tokens, half), preferred_element_type=F32
    ).astype(BF16)
    g_high = ring_z(s["ghi"], (short, long))
    for step in range(long):
        ring_step(x_low, step)
        ring_step(x_high, step)
        if step + 1 < long:
            ring_step(g_low, step)
            ring_step(g_high, step)
    arrive(list(x_low[7].values()) + list(x_high[7].values()))

    def z_at(p):
        step = (p + 1) // 2
        return (mz + nz // 2 + (1 - 2 * (p % 2)) * step + nz) % nz

    def rows_at(buf, p, columns):
        return buf[pl.ds(2 * z_at(p), 2), :, columns].reshape(2 * CAP, -1)

    pair = LANES // (2 * CAP)

    def rows_of(buf, g, columns):
        return jnp.concatenate([rows_at(buf, g * pair + i, columns) for i in range(pair)], axis=0)

    for load in loads:
        load.wait()
    every, low, high = slice(None), slice(0, half), slice(half, dim)

    def forward(g, _):
        cols = pl.ds(pl.multiple_of(g * LANES, LANES), LANES)
        x_hi = rows_of(s["xhi"], g, every)
        s["pre"][:, cols] = lax.dot_general(
            s["wgu"][:, low], rows_of(s["xlo"], g, every), TRANSPOSED_RIGHT, preferred_element_type=F32
        ) + lax.dot_general(
            s["wgu"][:, high], x_hi[:, :half], TRANSPOSED_RIGHT, preferred_element_type=F32
        )
        s["weight"][:, cols] = lax.dot_general(
            own_lane, x_hi[:, half:], TRANSPOSED_RIGHT, preferred_element_type=F32
        )
        return 0

    groups = nz // pair
    lax.fori_loop(0, groups, forward, 0)
    crossing = {}
    for g in range(groups - 1, -1, -1):
        if g == 0:
            ring_step(g_low, long - 1)
            ring_step(g_high, long - 1)
        for p in range(g * pair, (g + 1) * pair):
            distance = (nz // 2 + (1 - 2 * (p % 2)) * ((p + 1) // 2)) % nz
            arrive([g_low[7][distance], g_high[7][distance]])
        cols = slice(g * LANES, (g + 1) * LANES)
        back = lax.dot_general(
            s["wd"][:, low], rows_of(s["glo"], g, every), TRANSPOSED_RIGHT, preferred_element_type=F32
        ) + lax.dot_general(
            s["wd"][:, high], rows_of(s["ghi"], g, every), TRANSPOSED_RIGHT, preferred_element_type=F32
        )
        pre_gate, pre_up = s["pre"][:units, cols], s["pre"][units:, cols]
        weight = s["weight"][0:1, cols]
        sigmoid = 1.0 / (1.0 + jnp.exp(-pre_gate))
        silu = pre_gate * sigmoid
        active = silu * pre_up
        total = jnp.sum(active * back, axis=0, keepdims=True)
        total = jnp.transpose(jnp.broadcast_to(total, (LANES, LANES)))
        s["scaled"][:, cols] = (weight * active).astype(BF16)
        weighted = weight * back
        s["dcat"][:units, cols] = (
            weighted * pre_up * sigmoid * (1.0 + pre_gate * (1.0 - sigmoid))
        ).astype(BF16)
        s["dcat"][units:, cols] = (weighted * silu).astype(BF16)
        rows = lax.dot_general(
            s["dcat"][:, cols], s["wgu"][...], TRANSPOSED_LEFT, preferred_element_type=F32
        )
        for i in range(pair):
            z = z_at(g * pair + i)
            part = slice(2 * CAP * i, 2 * CAP * (i + 1))
            at = pl.ds(2 * z, 2)
            mine_rows, mine_total = rows[part].reshape(2, CAP, dim), total[part].reshape(2, CAP, LANES)
            s["rfull"][at, :, :dim] = mine_rows
            s["rhalf"][at, :, :dim] = mine_rows.astype(BF16)
            s["rfull"][at, :, dim:] = mine_total
            s["rhalf"][at, :, dim:] = split(mine_total)
            crossing[g * pair + i] = send(s["rhalf"].at[2 * z + 1 - core], s["sib"].at[z], sibling)

    tile = dim // 4

    def weights(n):
        cols = slice(n * tile, (n + 1) * tile)
        at = slice(n % 2 * tile, n % 2 * tile + tile)
        x_rows = jnp.concatenate([rows_at(s["xlo" if n < 2 else "xhi"], p, at) for p in range(nz)], axis=0)
        s["sums"][:, cols] = jnp.dot(s["dcat"][...], x_rows, preferred_element_type=F32)
        g_rows = jnp.concatenate([rows_at(s["glo" if n < 2 else "ghi"], p, at) for p in range(nz)], axis=0)
        s["sums_down"][:, cols] = jnp.dot(s["scaled"][...], g_rows, preferred_element_type=F32)

    sections = sections_of(dim)

    def piece(section, z):
        _, start, width, gate = section
        cols = slice(start, start + width)
        value = s["rfull"][2 * z + core, :, cols] + s["sib"][z, :, cols].astype(F32)
        if not gate:
            return value, None
        return value, s["rfull"][2 * z + core, :, dim:] + join(s["sib"][z, :, dim:])

    def add(value, ref, width):
        rows, gate_rows = value
        rows = rows + ref[:, :width].astype(F32)
        if gate_rows is not None:
            gate_rows = gate_rows + join(ref[:, width:])
        return rows, gate_rows

    crossed = set()

    def need(p):
        if p not in crossed:
            crossing[p].wait_recv()
            crossed.add(p)

    def place_of(distance):
        far = distance % nz - nz // 2
        return 2 * far if far >= 0 else -2 * far - 1

    last = {}
    for step in range(long):
        for n, section in enumerate(sections):
            hops = (long, short) if section[0] else (short, long)
            width = section[2]
            for side, sign in ((0, 1), (1, -1)):
                if step >= hops[side]:
                    continue
                if step:
                    last[n, side].wait_recv()
                distance = sign * (hops[side] - step)
                need(place_of(distance))
                value = piece(section, (mz + distance + nz) % nz)
                if step:
                    value = add(value, s[f"got{n}"].at[side, step - 1], width)
                put = s[f"put{n}"].at[side, step]
                put[:, :width] = value[0].astype(BF16)
                if section[3]:
                    put[:, width:] = split(value[1])
                last[n, side] = send(
                    put, s[f"got{n}"].at[side, step], at_z(up_z if side == 0 else down_z)
                )
        if step == 0:
            weights(0)
            weights(1)
        elif step < 3:
            weights(step + 1)
    for n in range(min(long, 3) + 1, 4):
        weights(n)
    stores = [
        pltpu.make_async_copy(s["sums"].at[pl.ds(0, units)], out_gate, s["lsem"].at[3]),
        pltpu.make_async_copy(s["sums"].at[pl.ds(units, units)], out_up, s["lsem"].at[4]),
        pltpu.make_async_copy(s["sums_down"], out_down, s["lsem"].at[5]),
    ]
    for store in stores:
        store.start()

    def back_to_tokens(place, rows):
        return lax.dot_general(place, rows, TRANSPOSED_LEFT, preferred_element_type=F32).astype(BF16)

    need(place_of(0))
    first, second = [], []
    for n, section in enumerate(sections):
        first_y, start, width, gate = section
        value = piece(section, mz)
        for side, hops in enumerate((long, short) if first_y else (short, long)):
            last[n, side].wait_recv()
            value = add(value, s[f"got{n}"].at[side, hops - 1], width)
        c, cr = s[f"c{n}"], s[f"cr{n}"]
        place = place_a if first_y else place_b
        c[:, :, :width] = back_to_tokens(place, value[0].astype(BF16)).reshape(c.shape[0], c.shape[1], width)
        if gate:
            lanes = lax.broadcasted_iota(jnp.int32, (CAP, LANES), 1)
            here = jnp.where(lanes % (LANES // 2) == mine, split(value[1]).astype(F32), 0.0).astype(BF16)
            c[:, :, width:] = back_to_tokens(place, here).reshape(c.shape[0], c.shape[1], LANES)
        if first_y:
            peers = [(my + d) % ny for d in range(1, ny)]
            first.append([send(c.at[y], cr.at[my], at_y(y)) for y in peers])
            cr[my] = c[my]
        else:
            peers = [(mx + d) % nx for d in range(1, nx)]
            first.append([send(c.at[x], cr.at[mx], at_x(x)) for x in peers])
            cr[mx] = c[mx]

    def total_of(buf):
        value = buf[0].astype(F32)
        for k in range(1, buf.shape[0]):
            value = value + buf[k].astype(F32)
        return value

    for n, section in enumerate(sections):
        arrive(first[n])
        e, er, wide = s[f"e{n}"], s[f"er{n}"], s[f"flat{n}"]
        wide[...] = total_of(s[f"cr{n}"])
        for k in range(e.shape[0]):
            e[k] = wide[2 * k : 2 * k + 2, :]
        if section[0]:
            peers = [(mx + d) % nx for d in range(1, nx)]
            second.append([send(e.at[x], er.at[mx], at_x(x)) for x in peers])
            er[mx] = e[mx]
        else:
            peers = [(my + d) % ny for d in range(1, ny)]
            second.append([send(e.at[y], er.at[my], at_y(y)) for y in peers])
            er[my] = e[my]

    for n, (_, start, width, gate) in enumerate(sections):
        arrive(second[n])
        final = total_of(s[f"er{n}"])
        out_in[:, start : start + width] = final[:, :width]
        if gate:
            grads = join(final[:, width:])
            inner = jnp.sum(spread * grads, axis=-1, keepdims=True)
            place = lax.broadcasted_iota(jnp.int32, (2, top), 1)
            result = jnp.zeros((2, top), F32)
            for k in range(top):
                own = jnp.sum(jnp.where(hits[k], grads, 0.0), axis=-1, keepdims=True)
                result = result + jnp.where(place == k, probs[:, k : k + 1] * (own - inner), 0.0)
            out_logits[...] = result
    for store in stores:
        store.wait()
    for copy in pending:
        copy.wait_send()


def hand_over(*refs):
    count = 5
    sources, results, stages = refs[:count], refs[count : 2 * count], refs[2 * count : 3 * count]
    load_sem, store_sem = refs[-2:]
    loads, stores = [], []
    for source, result, stage in zip(sources, results, stages):
        rows = source.shape[0]
        cuts = 3 if rows % 24 == 0 else 1
        for k in range(cuts):
            at, number = pl.ds(k * (rows // cuts), rows // cuts), len(loads)
            loads.append(pltpu.make_async_copy(source.at[at], stage.at[at], load_sem.at[number]))
            stores.append(pltpu.make_async_copy(stage.at[at], result.at[at], store_sem.at[number]))
    for load in loads:
        load.start()
    for load, store in zip(loads, stores):
        load.wait()
        store.start()
    for store in stores:
        store.wait()


def on_device(nx, ny, nz, tokens, grad_out, expert_ids, router_logits, w_gate, w_up, w_down):
    dim, units = w_gate.shape[1], w_gate.shape[2]
    shapes = scratch_of(nx, ny, nz, dim, units)
    spec = pl.BlockSpec(memory_space=pltpu.VMEM)
    anywhere = pl.BlockSpec(memory_space=pl.ANY)
    out_shape = [
        jax.ShapeDtypeStruct((2, dim), F32),
        jax.ShapeDtypeStruct(expert_ids.shape[1:], F32),
        jax.ShapeDtypeStruct((units, dim), F32),
        jax.ShapeDtypeStruct((units, dim), F32),
        jax.ShapeDtypeStruct((units, dim), F32),
    ]
    results = pl.pallas_call(
        functools.partial(kernel, nx, ny, nz, tuple(shapes)),
        out_shape=out_shape,
        in_specs=[spec] * 4 + [anywhere] * 3,
        out_specs=[spec] * 2 + [anywhere] * 3,
        scratch_shapes=list(shapes.values()),
        compiler_params=pltpu.CompilerParams(
            collective_id=0, has_side_effects=True, vmem_limit_bytes=56 * 1024 * 1024
        ),
    )(
        tokens[0], grad_out[0], expert_ids[0], router_logits[0],
        jnp.swapaxes(w_gate[0], 0, 1), jnp.swapaxes(w_up[0], 0, 1), w_down[0],
    )
    rows, logit_grads, sum_gate, sum_up, sum_down = pl.pallas_call(
        hand_over,
        out_shape=out_shape,
        in_specs=[anywhere] * 5,
        out_specs=[anywhere] * 5,
        scratch_shapes=[pltpu.VMEM(one.shape, F32) for one in out_shape]
        + [pltpu.SemaphoreType.DMA((11,))] * 2,
    )(*results)
    return (
        rows[None],
        logit_grads[None],
        jnp.swapaxes(sum_gate, 0, 1)[None],
        jnp.swapaxes(sum_up, 0, 1)[None],
        sum_down[None],
    )


def solution(mesh):
    side = math.isqrt(mesh.shape["expert"])
    nz = mesh.shape["hidden"] // 2
    token_spec, wide, tall = P("hidden", "expert", None), P("expert", None, "hidden"), P("expert", "hidden", None)
    return jax.shard_map(
        functools.partial(on_device, side, side, nz),
        mesh=mesh,
        in_specs=(token_spec,) * 4 + (wide, wide, tall),
        out_specs=(token_spec, token_spec, wide, wide, tall),
        check_vma=False,
    )
```

```python
import functools
import math

import jax
import jax.numpy as jnp
from jax import lax
from jax.experimental import pallas as pl
from jax.experimental.pallas import tpu as pltpu
from jax.sharding import PartitionSpec as P

MESH = pl.DeviceIdType.MESH
CAP = 32
LANES = 128
F32 = jnp.float32
BF16 = jnp.bfloat16
TRANSPOSED_RIGHT = (((1,), (1,)), ((), ()))
TRANSPOSED_LEFT = (((0,), (0,)), ((), ()))


def split(value):
    lane = lax.broadcasted_iota(jnp.int32, value.shape, value.ndim - 1)
    high = value.astype(BF16).astype(F32)
    return jnp.where(lane < LANES // 2, high, value - high).astype(BF16)


def join(parts):
    wide = parts.astype(F32)
    return wide + pltpu.roll(wide, LANES // 2, 1)


def sections_of(dim):
    half, quarter = dim // 2, dim // 4
    return [
        (True, 0, quarter, False),
        (False, half, quarter, True),
        (True, quarter, quarter, False),
        (False, half + quarter, quarter, False),
    ]


def scratch_of(nx, ny, nz, dim, units):
    vmem, dma = pltpu.VMEM, pltpu.SemaphoreType.DMA
    half, padded, long = dim // 2, dim + LANES, nz // 2
    wide = half + LANES
    flat = 2 * nz * CAP
    shapes = {
        "xa": vmem((2, wide), BF16), "xb": vmem((2, wide), BF16),
        "xa1": vmem((nx, 2, wide), BF16), "xb1": vmem((ny, 2, wide), BF16),
        "ga1": vmem((nx, 2, half), BF16), "gb1": vmem((ny, 2, half), BF16),
        "flat_a": vmem((2 * nx, wide), F32), "flat_b": vmem((2 * ny, wide), F32),
        "xa2": vmem((ny, 2 * nx, wide), BF16), "xb2": vmem((nx, 2 * ny, wide), BF16),
        "ga2": vmem((ny, 2 * nx, half), BF16), "gb2": vmem((nx, 2 * ny, half), BF16),
        "xlo": vmem((2 * nz, CAP, half), BF16), "xhi": vmem((2 * nz, CAP, wide), BF16),
        "glo": vmem((2 * nz, CAP, half), BF16), "ghi": vmem((2 * nz, CAP, half), BF16),
        "wgu": vmem((2 * units, dim), BF16), "wd": vmem((units, dim), BF16),
        "dcat": vmem((2 * units, flat), BF16), "scaled": vmem((units, flat), BF16),
        "rfull": vmem((2 * nz, CAP, padded), F32), "rhalf": vmem((2 * nz, CAP, padded), BF16),
        "sib": vmem((nz, CAP, padded), BF16),
        "sums": vmem((2 * units, dim), F32), "sums_down": vmem((units, dim), F32),
        "ssem": dma((256,)), "rsem": dma((256,)), "lsem": dma((8,)),
    }
    for n, (first_y, _, width, gate) in enumerate(sections_of(dim)):
        size = width + (LANES if gate else 0)
        one, two = (ny, nx) if first_y else (nx, ny)
        shapes[f"put{n}"] = vmem((2, long, CAP, size), BF16)
        shapes[f"got{n}"] = vmem((2, long, CAP, size), BF16)
        shapes[f"c{n}"] = vmem((one, 2 * two, size), BF16)
        shapes[f"cr{n}"] = vmem((one, 2 * two, size), BF16)
        shapes[f"e{n}"] = vmem((two, 2, size), F32)
        shapes[f"er{n}"] = vmem((two, 2, size), F32)
        shapes[f"flat{n}"] = vmem((2 * two, size), F32)
    return shapes


def kernel(
    nx, ny, nz, names,
    tok, grd, ids, logits, wg, wu, wdn,
    out_in, out_logits, out_gate, out_up, out_down, *scratch,
):
    s = dict(zip(names, scratch))
    mine = lax.axis_index("expert")
    hid = lax.axis_index("hidden")
    mx, my = mine // ny, mine % ny
    mz, core = hid // 2, hid % 2
    units, dim = wdn.shape
    top = ids.shape[1]
    half = dim // 2
    tokens = 2 * nx * ny
    long, short = nz // 2, nz // 2 - 1

    def at_x(x):
        return {"expert": x * ny + my, "hidden": hid}

    def at_y(y):
        return {"expert": mx * ny + y, "hidden": hid}

    def at_z(z):
        return {"expert": mine, "hidden": 2 * z + core}

    sibling = {"expert": mine, "hidden": 2 * mz + 1 - core}
    up_z, down_z = (mz + 1) % nz, (mz + nz - 1) % nz
    pending = []

    def send(src, dst, device):
        number = len(pending)
        copy = pltpu.make_async_remote_copy(
            src_ref=src, dst_ref=dst, send_sem=s["ssem"].at[number], recv_sem=s["rsem"].at[number],
            device_id=device, device_id_type=MESH,
        )
        copy.start()
        pending.append(copy)
        return copy

    def arrive(copies):
        for copy in copies:
            copy.wait_recv()

    barrier = pltpu.get_barrier_semaphore()
    greet = [at_x((mx + d) % nx) for d in range(1, nx)]
    greet += [at_y((my + d) % ny) for d in range(1, ny)]
    greet += [at_z(up_z), at_z(down_z), sibling]
    for device in greet:
        pl.semaphore_signal(barrier, inc=1, device_id=device, device_id_type=MESH)

    loads = [
        pltpu.make_async_copy(wg, s["wgu"].at[pl.ds(0, units)], s["lsem"].at[0]),
        pltpu.make_async_copy(wu, s["wgu"].at[pl.ds(units, units)], s["lsem"].at[1]),
        pltpu.make_async_copy(wdn, s["wd"], s["lsem"].at[2]),
    ]
    for load in loads:
        load.start()

    raised = jnp.exp(logits[...])
    probs = raised / jnp.sum(raised, axis=-1, keepdims=True)
    lane_of = lax.broadcasted_iota(jnp.int32, (2, LANES), 1)
    hits = [lane_of == ids[:, k : k + 1] for k in range(top)]
    spread = jnp.zeros((2, LANES), F32)
    for k in range(top):
        spread = spread + jnp.where(hits[k], probs[:, k : k + 1], 0.0)
    table = spread.astype(BF16)
    s["xa"][:, :half] = tok[:, :half]
    s["xb"][:, :half] = tok[:, half:]
    s["xa"][:, half:] = table
    s["xb"][:, half:] = table
    pl.semaphore_wait(barrier, len(greet))

    def spread_x(src, dst):
        return [send(src, dst.at[mx], at_x((mx + d) % nx)) for d in range(1, nx)]

    def spread_y(src, dst):
        return [send(src, dst.at[my], at_y((my + d) % ny)) for d in range(1, ny)]

    xa = spread_x(s["xa"], s["xa1"])
    xb = spread_y(s["xb"], s["xb1"])
    ga = spread_x(grd.at[:, pl.ds(0, half)], s["ga1"])
    gb = spread_y(grd.at[:, pl.ds(half, half)], s["gb1"])
    s["xa1"][mx] = s["xa"][...]
    s["xb1"][my] = s["xb"][...]
    s["ga1"][mx] = grd[:, :half]
    s["gb1"][my] = grd[:, half:]

    def flatten(blocks, wide):
        count, _, width = blocks.shape
        for k in range(count):
            wide[2 * k : 2 * k + 2, :width] = blocks[k].astype(F32)
        return wide[:, :width].astype(BF16)

    def ring_start(buf, at, place, size, hops, up, down, across):
        own = buf.at[at(place)]
        waits = [send(own, own, device) if hop else None for hop, device in zip(hops, (up, down))]
        over = {0: send(own, own, sibling)} if across else {}
        return buf, at, place, size, hops, (up, down), waits, over, across

    def ring_step(ring, step):
        buf, at, place, size, hops, devices, waits, over, across = ring
        for side in (0, 1) if hops[0] >= hops[1] else (1, 0):
            if step >= hops[side]:
                continue
            distance = -(step + 1) if side == 0 else step + 1
            waits[side].wait_recv()
            block = buf.at[at((place + distance + size) % size)]
            if step + 1 < hops[side]:
                waits[side] = send(block, block, devices[side])
            if across:
                over[distance % size] = send(block, block, sibling)

    def ring_z(buf, hops):
        return ring_start(buf, lambda z: 2 * z + core, mz, nz, hops, at_z(up_z), at_z(down_z), True)

    def hand_start(buf, at, size, device):
        own = buf.at[at]
        far = range(1, size) if size != 8 else (2, 6, 1, 7)
        return {-d % size: send(own, own, device((at + d) % size)) for d in far}

    def hand_on(copies, buf, at, size, device, upward):
        if size != 8:
            return
        for toward in (1, -1):
            from_here = -2 * toward % size
            copies.pop(from_here).wait_recv()
            block = buf.at[(at - 2 * toward + size) % size]
            copies[-3 * toward % size] = send(block, block, device((at + toward + size) % size))
            if (toward > 0) == upward:
                copies[4] = send(block, block, device((at + 2 * toward + size) % size))

    along_y, along_x = (my, ny, at_y), (mx, nx, at_x)
    arrive(xa)
    s["xa2"][my] = flatten(s["xa1"], s["flat_a"])
    xa = hand_start(s["xa2"], *along_y)
    arrive(xb)
    s["xb2"][mx] = flatten(s["xb1"], s["flat_b"])
    xb = hand_start(s["xb2"], *along_x)
    arrive(ga)
    s["ga2"][my] = flatten(s["ga1"], s["flat_a"])
    arrive(gb)
    s["gb2"][mx] = flatten(s["gb1"], s["flat_b"])
    hand_on(xa, s["xa2"], *along_y, True)
    hand_on(xb, s["xb2"], *along_x, True)
    ga = hand_start(s["ga2"], *along_y)
    gb = hand_start(s["gb2"], *along_x)

    own_lane = jnp.where(lax.broadcasted_iota(jnp.int32, (8, LANES), 1) == mine, 1.0, 0.0).astype(BF16)

    def order_a(t):
        return t

    def order_b(t):
        xx, yy, jj = t // (2 * ny), (t // 2) % ny, t % 2
        return (yy * nx + xx) * 2 + jj

    def placing_of(gates, order):
        gate = lax.dot_general(own_lane, gates, TRANSPOSED_RIGHT, preferred_element_type=F32)
        picked = jnp.where(gate > 0.0, 1.0, 0.0)
        before = order(lax.broadcasted_iota(jnp.int32, (tokens, tokens), 0))
        after = order(lax.broadcasted_iota(jnp.int32, (tokens, tokens), 1))
        upto = jnp.where(before <= after, 1.0, 0.0).astype(BF16)
        rank = jnp.dot(picked.astype(BF16), upto, preferred_element_type=F32) - 1.0
        rank = jnp.where(picked > 0.0, rank, -1.0)
        slot = lax.broadcasted_iota(jnp.int32, (CAP, tokens), 0).astype(F32)
        return jnp.where(rank[0:1, :] == slot, 1.0, 0.0).astype(BF16)

    arrive(xa.values())
    wide_a = s["xa2"][...].reshape(tokens, half + LANES)
    place_a = placing_of(wide_a[:, half:], order_a)
    s["xlo"][hid] = jnp.dot(place_a, wide_a[:, :half], preferred_element_type=F32).astype(BF16)
    x_low = ring_z(s["xlo"], (long, short))
    arrive(xb.values())
    wide_b = s["xb2"][...].reshape(tokens, half + LANES)
    place_b = placing_of(wide_b[:, half:], order_b)
    s["xhi"][hid] = jnp.dot(place_b, wide_b, preferred_element_type=F32).astype(BF16)
    x_high = ring_z(s["xhi"], (short, long))
    hand_on(ga, s["ga2"], *along_y, False)
    hand_on(gb, s["gb2"], *along_x, False)
    arrive(ga.values())
    s["glo"][hid] = jnp.dot(
        place_a, s["ga2"][...].reshape(tokens, half), preferred_element_type=F32
    ).astype(BF16)
    g_low = ring_z(s["glo"], (long, short))
    arrive(gb.values())
    s["ghi"][hid] = jnp.dot(
        place_b, s["gb2"][...].reshape(tokens, half), preferred_element_type=F32
    ).astype(BF16)
    g_high = ring_z(s["ghi"], (short, long))
    def z_at(p):
        step = (p + 1) // 2
        return (mz + nz // 2 + (1 - 2 * (p % 2)) * step + nz) % nz

    def rows_at(buf, p, columns):
        return buf[pl.ds(2 * z_at(p), 2), :, columns].reshape(2 * CAP, -1)

    pair = LANES // (2 * CAP)

    def rows_of(buf, g, columns):
        return jnp.concatenate([rows_at(buf, g * pair + i, columns) for i in range(pair)], axis=0)

    every, low, high = slice(None), slice(0, half), slice(half, dim)
    groups = nz // pair
    crossing = {}

    def compute(g):
        for p in range(g * pair, (g + 1) * pair):
            distance = (nz // 2 + (1 - 2 * (p % 2)) * ((p + 1) // 2)) % nz
            arrive([ring[7][distance] for ring in (x_low, x_high, g_low, g_high)])
        cols = slice(g * LANES, (g + 1) * LANES)
        x_hi = rows_of(s["xhi"], g, every)
        pre = lax.dot_general(
            s["wgu"][:, low], rows_of(s["xlo"], g, every), TRANSPOSED_RIGHT, preferred_element_type=F32
        ) + lax.dot_general(
            s["wgu"][:, high], x_hi[:, :half], TRANSPOSED_RIGHT, preferred_element_type=F32
        )
        weight = lax.dot_general(
            own_lane, x_hi[:, half:], TRANSPOSED_RIGHT, preferred_element_type=F32
        )[0:1, :]
        back = lax.dot_general(
            s["wd"][:, low], rows_of(s["glo"], g, every), TRANSPOSED_RIGHT, preferred_element_type=F32
        ) + lax.dot_general(
            s["wd"][:, high], rows_of(s["ghi"], g, every), TRANSPOSED_RIGHT, preferred_element_type=F32
        )
        pre_gate, pre_up = pre[:units], pre[units:]
        sigmoid = 1.0 / (1.0 + jnp.exp(-pre_gate))
        silu = pre_gate * sigmoid
        active = silu * pre_up
        total = jnp.sum(active * back, axis=0, keepdims=True)
        total = jnp.transpose(jnp.broadcast_to(total, (LANES, LANES)))
        s["scaled"][:, cols] = (weight * active).astype(BF16)
        weighted = weight * back
        s["dcat"][:units, cols] = (
            weighted * pre_up * sigmoid * (1.0 + pre_gate * (1.0 - sigmoid))
        ).astype(BF16)
        s["dcat"][units:, cols] = (weighted * silu).astype(BF16)
        rows = lax.dot_general(
            s["dcat"][:, cols], s["wgu"][...], TRANSPOSED_LEFT, preferred_element_type=F32
        )
        for i in range(pair):
            z = z_at(g * pair + i)
            part = slice(2 * CAP * i, 2 * CAP * (i + 1))
            at = pl.ds(2 * z, 2)
            mine_rows, mine_total = rows[part].reshape(2, CAP, dim), total[part].reshape(2, CAP, LANES)
            s["rfull"][at, :, :dim] = mine_rows
            s["rhalf"][at, :, :dim] = mine_rows.astype(BF16)
            s["rfull"][at, :, dim:] = mine_total
            s["rhalf"][at, :, dim:] = split(mine_total)
            crossing[g * pair + i] = send(s["rhalf"].at[2 * z + 1 - core], s["sib"].at[z], sibling)

    for load in loads:
        load.wait()
    for step in range(long):
        ring_step(x_low, step)
        ring_step(x_high, step)
        ring_step(g_low, step)
        ring_step(g_high, step)
        if step >= 1:
            compute(groups - step)
    for g in range(groups - long, -1, -1):
        compute(g)

    tile = dim // 4

    def weights(n):
        cols = slice(n * tile, (n + 1) * tile)
        at = slice(n % 2 * tile, n % 2 * tile + tile)
        x_rows = jnp.concatenate([rows_at(s["xlo" if n < 2 else "xhi"], p, at) for p in range(nz)], axis=0)
        s["sums"][:, cols] = jnp.dot(s["dcat"][...], x_rows, preferred_element_type=F32)
        g_rows = jnp.concatenate([rows_at(s["glo" if n < 2 else "ghi"], p, at) for p in range(nz)], axis=0)
        s["sums_down"][:, cols] = jnp.dot(s["scaled"][...], g_rows, preferred_element_type=F32)

    sections = sections_of(dim)

    def piece(section, z):
        _, start, width, gate = section
        cols = slice(start, start + width)
        value = s["rfull"][2 * z + core, :, cols] + s["sib"][z, :, cols].astype(F32)
        if not gate:
            return value, None
        return value, s["rfull"][2 * z + core, :, dim:] + join(s["sib"][z, :, dim:])

    def add(value, ref, width):
        rows, gate_rows = value
        rows = rows + ref[:, :width].astype(F32)
        if gate_rows is not None:
            gate_rows = gate_rows + join(ref[:, width:])
        return rows, gate_rows

    crossed = set()

    def need(p):
        if p not in crossed:
            crossing[p].wait_recv()
            crossed.add(p)

    def place_of(distance):
        far = distance % nz - nz // 2
        return 2 * far if far >= 0 else -2 * far - 1

    last, first, second = {}, {}, {}

    def reduce_step(n, step):
        section = sections[n]
        hops = (long, short) if section[0] else (short, long)
        width = section[2]
        for side, sign in ((0, 1), (1, -1)):
            if step >= hops[side]:
                continue
            if step:
                last[n, side].wait_recv()
            distance = sign * (hops[side] - step)
            need(place_of(distance))
            value = piece(section, (mz + distance + nz) % nz)
            if step:
                value = add(value, s[f"got{n}"].at[side, step - 1], width)
            put = s[f"put{n}"].at[side, step]
            put[:, :width] = value[0].astype(BF16)
            if section[3]:
                put[:, width:] = split(value[1])
            last[n, side] = send(
                put, s[f"got{n}"].at[side, step], at_z(up_z if side == 0 else down_z)
            )

    def back_to_tokens(place, rows):
        return lax.dot_general(place, rows, TRANSPOSED_LEFT, preferred_element_type=F32).astype(BF16)

    def reduce_end(n):
        first_y, start, width, gate = section = sections[n]
        need(place_of(0))
        value = piece(section, mz)
        for side, hops in enumerate((long, short) if first_y else (short, long)):
            if hops:
                last[n, side].wait_recv()
                value = add(value, s[f"got{n}"].at[side, hops - 1], width)
        c, cr = s[f"c{n}"], s[f"cr{n}"]
        place = place_a if first_y else place_b
        c[:, :, :width] = back_to_tokens(place, value[0].astype(BF16)).reshape(c.shape[0], c.shape[1], width)
        if gate:
            lanes = lax.broadcasted_iota(jnp.int32, (CAP, LANES), 1)
            here = jnp.where(lanes % (LANES // 2) == mine, split(value[1]).astype(F32), 0.0).astype(BF16)
            c[:, :, width:] = back_to_tokens(place, here).reshape(c.shape[0], c.shape[1], LANES)
        if first_y:
            peers = [(my + d) % ny for d in sorted(range(1, ny), key=lambda d: -min(d, ny - d))]
            first[n] = [send(c.at[y], cr.at[my], at_y(y)) for y in peers]
            cr[my] = c[my]
        else:
            peers = [(mx + d) % nx for d in sorted(range(1, nx), key=lambda d: -min(d, nx - d))]
            first[n] = [send(c.at[x], cr.at[mx], at_x(x)) for x in peers]
            cr[mx] = c[mx]

    for turn in range(long + 1):
        for n in range(len(sections)):
            if turn < long:
                reduce_step(n, turn)
            else:
                reduce_end(n)
        if turn < 4:
            weights(turn)
        if turn == min(3, long):
            for n in range(turn + 1, 4):
                weights(n)
            stores = [
                pltpu.make_async_copy(s["sums"].at[pl.ds(0, units)], out_gate, s["lsem"].at[3]),
                pltpu.make_async_copy(s["sums"].at[pl.ds(units, units)], out_up, s["lsem"].at[4]),
                pltpu.make_async_copy(s["sums_down"], out_down, s["lsem"].at[5]),
            ]
            for store in stores:
                store.start()

    def total_of(buf):
        value = buf[0].astype(F32)
        for k in range(1, buf.shape[0]):
            value = value + buf[k].astype(F32)
        return value

    for n, section in enumerate(sections):
        arrive(first[n])
        e, er, wide = s[f"e{n}"], s[f"er{n}"], s[f"flat{n}"]
        wide[...] = total_of(s[f"cr{n}"])
        for k in range(e.shape[0]):
            e[k] = wide[2 * k : 2 * k + 2, :]
        if section[0]:
            peers = [(mx + d) % nx for d in sorted(range(1, nx), key=lambda d: -min(d, nx - d))]
            second[n] = [send(e.at[x], er.at[mx], at_x(x)) for x in peers]
            er[mx] = e[mx]
        else:
            peers = [(my + d) % ny for d in sorted(range(1, ny), key=lambda d: -min(d, ny - d))]
            second[n] = [send(e.at[y], er.at[my], at_y(y)) for y in peers]
            er[my] = e[my]

    for n, (_, start, width, gate) in enumerate(sections):
        arrive(second[n])
        final = total_of(s[f"er{n}"])
        out_in[:, start : start + width] = final[:, :width]
        if gate:
            grads = join(final[:, width:])
            inner = jnp.sum(spread * grads, axis=-1, keepdims=True)
            place = lax.broadcasted_iota(jnp.int32, (2, top), 1)
            result = jnp.zeros((2, top), F32)
            for k in range(top):
                own = jnp.sum(jnp.where(hits[k], grads, 0.0), axis=-1, keepdims=True)
                result = result + jnp.where(place == k, probs[:, k : k + 1] * (own - inner), 0.0)
            out_logits[...] = result
    for store in stores:
        store.wait()
    for copy in pending:
        copy.wait_send()


def hand_over(*refs):
    count = 5
    sources, results, stages = refs[:count], refs[count : 2 * count], refs[2 * count : 3 * count]
    load_sem, store_sem = refs[-2:]
    loads, stores = [], []
    for source, result, stage in zip(sources, results, stages):
        rows = source.shape[0]
        cuts = 3 if rows % 24 == 0 else 1
        for k in range(cuts):
            at, number = pl.ds(k * (rows // cuts), rows // cuts), len(loads)
            loads.append(pltpu.make_async_copy(source.at[at], stage.at[at], load_sem.at[number]))
            stores.append(pltpu.make_async_copy(stage.at[at], result.at[at], store_sem.at[number]))
    for load in loads:
        load.start()
    for load, store in zip(loads, stores):
        load.wait()
        store.start()
    for store in stores:
        store.wait()


def on_device(nx, ny, nz, tokens, grad_out, expert_ids, router_logits, w_gate, w_up, w_down):
    dim, units = w_gate.shape[1], w_gate.shape[2]
    shapes = scratch_of(nx, ny, nz, dim, units)
    spec = pl.BlockSpec(memory_space=pltpu.VMEM)
    anywhere = pl.BlockSpec(memory_space=pl.ANY)
    out_shape = [
        jax.ShapeDtypeStruct((2, dim), F32),
        jax.ShapeDtypeStruct(expert_ids.shape[1:], F32),
        jax.ShapeDtypeStruct((units, dim), F32),
        jax.ShapeDtypeStruct((units, dim), F32),
        jax.ShapeDtypeStruct((units, dim), F32),
    ]
    results = pl.pallas_call(
        functools.partial(kernel, nx, ny, nz, tuple(shapes)),
        out_shape=out_shape,
        in_specs=[spec] * 4 + [anywhere] * 3,
        out_specs=[spec] * 2 + [anywhere] * 3,
        scratch_shapes=list(shapes.values()),
        compiler_params=pltpu.CompilerParams(
            collective_id=0, has_side_effects=True, vmem_limit_bytes=56 * 1024 * 1024
        ),
    )(
        tokens[0], grad_out[0], expert_ids[0], router_logits[0],
        jnp.swapaxes(w_gate[0], 0, 1), jnp.swapaxes(w_up[0], 0, 1), w_down[0],
    )
    rows, logit_grads, sum_gate, sum_up, sum_down = pl.pallas_call(
        hand_over,
        out_shape=out_shape,
        in_specs=[anywhere] * 5,
        out_specs=[anywhere] * 5,
        scratch_shapes=[pltpu.VMEM(one.shape, F32) for one in out_shape]
        + [pltpu.SemaphoreType.DMA((11,))] * 2,
    )(*results)
    return (
        rows[None],
        logit_grads[None],
        jnp.swapaxes(sum_gate, 0, 1)[None],
        jnp.swapaxes(sum_up, 0, 1)[None],
        sum_down[None],
    )


def solution(mesh):
    side = math.isqrt(mesh.shape["expert"])
    nz = mesh.shape["hidden"] // 2
    token_spec, wide, tall = P("hidden", "expert", None), P("expert", None, "hidden"), P("expert", "hidden", None)
    return jax.shard_map(
        functools.partial(on_device, side, side, nz),
        mesh=mesh,
        in_specs=(token_spec,) * 4 + (wide, wide, tall),
        out_specs=(token_spec, token_spec, wide, wide, tall),
        check_vma=False,
    )
```

```python
import functools
import math

import jax
import jax.numpy as jnp
from jax import lax
from jax.experimental import pallas as pl
from jax.experimental.pallas import tpu as pltpu
from jax.sharding import PartitionSpec as P

MESH = pl.DeviceIdType.MESH
CAP = 32
LANES = 128
F32 = jnp.float32
BF16 = jnp.bfloat16
TRANSPOSED_RIGHT = (((1,), (1,)), ((), ()))
TRANSPOSED_LEFT = (((0,), (0,)), ((), ()))


def split(value):
    lane = lax.broadcasted_iota(jnp.int32, value.shape, value.ndim - 1)
    high = value.astype(BF16).astype(F32)
    return jnp.where(lane < LANES // 2, high, value - high).astype(BF16)


def join(parts):
    wide = parts.astype(F32)
    return wide + pltpu.roll(wide, LANES // 2, 1)


def sections_of(dim):
    half, quarter = dim // 2, dim // 4
    return [
        (True, 0, quarter, False),
        (False, half, quarter, True),
        (True, quarter, quarter, False),
        (False, half + quarter, quarter, False),
    ]


def scratch_of(nx, ny, nz, dim, units):
    vmem, dma = pltpu.VMEM, pltpu.SemaphoreType.DMA
    half, padded, long = dim // 2, dim + LANES, nz // 2
    wide = half + LANES
    flat = 2 * nz * CAP
    shapes = {
        "xa": vmem((2, padded), BF16), "xb": vmem((2, padded), BF16),
        "xa1": vmem((nx, 2, padded), BF16), "xb1": vmem((ny, 2, padded), BF16),
        "flat_a": vmem((2 * nx, padded), F32), "flat_b": vmem((2 * ny, padded), F32),
        "xa2": vmem((ny, 2 * nx, wide), BF16), "xb2": vmem((nx, 2 * ny, wide), BF16),
        "ga2": vmem((ny, 2 * nx, half), BF16), "gb2": vmem((nx, 2 * ny, half), BF16),
        "xlo": vmem((2 * nz, CAP, half), BF16), "xhi": vmem((2 * nz, CAP, wide), BF16),
        "glo": vmem((2 * nz, CAP, half), BF16), "ghi": vmem((2 * nz, CAP, half), BF16),
        "wgu": vmem((2 * units, dim), BF16), "wd": vmem((units, dim), BF16),
        "dcat": vmem((2 * units, flat), BF16), "scaled": vmem((units, flat), BF16),
        "rfull": vmem((2 * nz, CAP, padded), F32), "rhalf": vmem((2 * nz, CAP, padded), BF16),
        "sib": vmem((nz, CAP, padded), BF16),
        "sums": vmem((2 * units, dim), F32), "sums_down": vmem((units, dim), F32),
        "ssem": dma((256,)), "rsem": dma((256,)), "lsem": dma((8,)),
    }
    for n, (first_y, _, width, gate) in enumerate(sections_of(dim)):
        size = width + (LANES if gate else 0)
        one, two = (ny, nx) if first_y else (nx, ny)
        shapes[f"put{n}"] = vmem((2, long, CAP, size), BF16)
        shapes[f"got{n}"] = vmem((2, long, CAP, size), BF16)
        shapes[f"c{n}"] = vmem((one, 2 * two, size), BF16)
        shapes[f"cr{n}"] = vmem((one, 2 * two, size), BF16)
        shapes[f"e{n}"] = vmem((two, 2, size), F32)
        shapes[f"er{n}"] = vmem((two, 2, size), F32)
        shapes[f"flat{n}"] = vmem((2 * two, size), F32)
    return shapes


def kernel(
    nx, ny, nz, names,
    tok, grd, ids, logits, wg, wu, wdn,
    out_in, out_logits, out_gate, out_up, out_down, *scratch,
):
    s = dict(zip(names, scratch))
    mine = lax.axis_index("expert")
    hid = lax.axis_index("hidden")
    mx, my = mine // ny, mine % ny
    mz, core = hid // 2, hid % 2
    units, dim = wdn.shape
    top = ids.shape[1]
    half = dim // 2
    wide = half + LANES
    tokens = 2 * nx * ny
    long, short = nz // 2, nz // 2 - 1

    def at_x(x):
        return {"expert": x * ny + my, "hidden": hid}

    def at_y(y):
        return {"expert": mx * ny + y, "hidden": hid}

    def at_z(z):
        return {"expert": mine, "hidden": 2 * z + core}

    sibling = {"expert": mine, "hidden": 2 * mz + 1 - core}
    up_z, down_z = (mz + 1) % nz, (mz + nz - 1) % nz
    pending = []

    def send(src, dst, device):
        number = len(pending)
        copy = pltpu.make_async_remote_copy(
            src_ref=src, dst_ref=dst, send_sem=s["ssem"].at[number], recv_sem=s["rsem"].at[number],
            device_id=device, device_id_type=MESH,
        )
        copy.start()
        pending.append(copy)
        return copy

    def arrive(copies):
        for copy in copies:
            copy.wait_recv()

    barrier = pltpu.get_barrier_semaphore()
    greet = [at_x((mx + d) % nx) for d in range(1, nx)]
    greet += [at_y((my + d) % ny) for d in range(1, ny)]
    greet += [at_z(up_z), at_z(down_z), sibling]
    for device in greet:
        pl.semaphore_signal(barrier, inc=1, device_id=device, device_id_type=MESH)

    loads = [
        pltpu.make_async_copy(wg, s["wgu"].at[pl.ds(0, units)], s["lsem"].at[0]),
        pltpu.make_async_copy(wu, s["wgu"].at[pl.ds(units, units)], s["lsem"].at[1]),
        pltpu.make_async_copy(wdn, s["wd"], s["lsem"].at[2]),
    ]
    for load in loads:
        load.start()

    raised = jnp.exp(logits[...])
    probs = raised / jnp.sum(raised, axis=-1, keepdims=True)
    lane_of = lax.broadcasted_iota(jnp.int32, (2, LANES), 1)
    hits = [lane_of == ids[:, k : k + 1] for k in range(top)]
    spread = jnp.zeros((2, LANES), F32)
    for k in range(top):
        spread = spread + jnp.where(hits[k], probs[:, k : k + 1], 0.0)
    table = spread.astype(BF16)
    s["xa"][:, :half] = tok[:, :half]
    s["xb"][:, :half] = tok[:, half:]
    s["xa"][:, half:wide] = table
    s["xb"][:, half:wide] = table
    s["xa"][:, wide:] = grd[:, :half]
    s["xb"][:, wide:] = grd[:, half:]
    pl.semaphore_wait(barrier, len(greet))

    def spread_x(src, dst):
        return [send(src, dst.at[mx], at_x((mx + d) % nx)) for d in range(1, nx)]

    def spread_y(src, dst):
        return [send(src, dst.at[my], at_y((my + d) % ny)) for d in range(1, ny)]

    xa = spread_x(s["xa"], s["xa1"])
    xb = spread_y(s["xb"], s["xb1"])
    s["xa1"][mx] = s["xa"][...]
    s["xb1"][my] = s["xb"][...]

    def flatten(blocks, flat):
        for k in range(blocks.shape[0]):
            flat[2 * k : 2 * k + 2, :] = blocks[k].astype(F32)
        return flat[...].astype(BF16)

    def ring_start(buf, at, place, size, hops, up, down, across):
        own = buf.at[at(place)]
        waits = [send(own, own, device) if hop else None for hop, device in zip(hops, (up, down))]
        over = {0: send(own, own, sibling)} if across else {}
        return buf, at, place, size, hops, (up, down), waits, over, across

    def ring_step(ring, step):
        buf, at, place, size, hops, devices, waits, over, across = ring
        for side in (0, 1) if hops[0] >= hops[1] else (1, 0):
            if step >= hops[side]:
                continue
            distance = -(step + 1) if side == 0 else step + 1
            waits[side].wait_recv()
            block = buf.at[at((place + distance + size) % size)]
            if step + 1 < hops[side]:
                waits[side] = send(block, block, devices[side])
            if across:
                over[distance % size] = send(block, block, sibling)

    def ring_z(buf, hops):
        return ring_start(buf, lambda z: 2 * z + core, mz, nz, hops, at_z(up_z), at_z(down_z), True)

    def hand_start(buf, at, size, device):
        own = buf.at[at]
        far = range(1, size) if size != 8 else (2, 6, 1, 7)
        return {-d % size: send(own, own, device((at + d) % size)) for d in far}

    def hand_on(copies, buf, at, size, device, upward):
        if size != 8:
            return
        for toward in (1, -1):
            from_here = -2 * toward % size
            copies.pop(from_here).wait_recv()
            block = buf.at[(at - 2 * toward + size) % size]
            copies[-3 * toward % size] = send(block, block, device((at + toward + size) % size))
            if (toward > 0) == upward:
                copies[4] = send(block, block, device((at + 2 * toward + size) % size))

    along_y, along_x = (my, ny, at_y), (mx, nx, at_x)
    arrive(xa)
    flat = flatten(s["xa1"], s["flat_a"])
    s["xa2"][my] = flat[:, :wide]
    s["ga2"][my] = flat[:, wide:]
    xa = hand_start(s["xa2"], *along_y)
    arrive(xb)
    flat = flatten(s["xb1"], s["flat_b"])
    s["xb2"][mx] = flat[:, :wide]
    s["gb2"][mx] = flat[:, wide:]
    xb = hand_start(s["xb2"], *along_x)
    hand_on(xa, s["xa2"], *along_y, True)
    hand_on(xb, s["xb2"], *along_x, True)
    ga = hand_start(s["ga2"], *along_y)
    gb = hand_start(s["gb2"], *along_x)

    own_lane = jnp.where(lax.broadcasted_iota(jnp.int32, (8, LANES), 1) == mine, 1.0, 0.0).astype(BF16)

    def order_a(t):
        return t

    def order_b(t):
        xx, yy, jj = t // (2 * ny), (t // 2) % ny, t % 2
        return (yy * nx + xx) * 2 + jj

    def placing_of(gates, order):
        gate = lax.dot_general(own_lane, gates, TRANSPOSED_RIGHT, preferred_element_type=F32)
        picked = jnp.where(gate > 0.0, 1.0, 0.0)
        before = order(lax.broadcasted_iota(jnp.int32, (tokens, tokens), 0))
        after = order(lax.broadcasted_iota(jnp.int32, (tokens, tokens), 1))
        upto = jnp.where(before <= after, 1.0, 0.0).astype(BF16)
        rank = jnp.dot(picked.astype(BF16), upto, preferred_element_type=F32) - 1.0
        rank = jnp.where(picked > 0.0, rank, -1.0)
        slot = lax.broadcasted_iota(jnp.int32, (CAP, tokens), 0).astype(F32)
        return jnp.where(rank[0:1, :] == slot, 1.0, 0.0).astype(BF16)

    arrive(xa.values())
    wide_a = s["xa2"][...].reshape(tokens, half + LANES)
    place_a = placing_of(wide_a[:, half:], order_a)
    s["xlo"][hid] = jnp.dot(place_a, wide_a[:, :half], preferred_element_type=F32).astype(BF16)
    x_low = ring_z(s["xlo"], (long, short))
    arrive(xb.values())
    wide_b = s["xb2"][...].reshape(tokens, half + LANES)
    place_b = placing_of(wide_b[:, half:], order_b)
    s["xhi"][hid] = jnp.dot(place_b, wide_b, preferred_element_type=F32).astype(BF16)
    x_high = ring_z(s["xhi"], (short, long))
    hand_on(ga, s["ga2"], *along_y, False)
    hand_on(gb, s["gb2"], *along_x, False)
    ring_step(x_low, 0)
    ring_step(x_high, 0)
    arrive(ga.values())
    s["glo"][hid] = jnp.dot(
        place_a, s["ga2"][...].reshape(tokens, half), preferred_element_type=F32
    ).astype(BF16)
    g_low = ring_z(s["glo"], (long, short))
    arrive(gb.values())
    s["ghi"][hid] = jnp.dot(
        place_b, s["gb2"][...].reshape(tokens, half), preferred_element_type=F32
    ).astype(BF16)
    g_high = ring_z(s["ghi"], (short, long))
    def z_at(p):
        step = (p + 1) // 2
        return (mz + nz // 2 + (1 - 2 * (p % 2)) * step + nz) % nz

    def rows_at(buf, p, columns):
        return buf[pl.ds(2 * z_at(p), 2), :, columns].reshape(2 * CAP, -1)

    pair = LANES // (2 * CAP)

    def rows_of(buf, g, columns):
        return jnp.concatenate([rows_at(buf, g * pair + i, columns) for i in range(pair)], axis=0)

    every, low, high = slice(None), slice(0, half), slice(half, dim)
    groups = nz // pair
    crossing = {}

    def compute(g):
        for p in range(g * pair, (g + 1) * pair):
            distance = (nz // 2 + (1 - 2 * (p % 2)) * ((p + 1) // 2)) % nz
            arrive([ring[7][distance] for ring in (x_low, x_high, g_low, g_high)])
        cols = slice(g * LANES, (g + 1) * LANES)
        x_hi = rows_of(s["xhi"], g, every)
        pre = lax.dot_general(
            s["wgu"][:, low], rows_of(s["xlo"], g, every), TRANSPOSED_RIGHT, preferred_element_type=F32
        ) + lax.dot_general(
            s["wgu"][:, high], x_hi[:, :half], TRANSPOSED_RIGHT, preferred_element_type=F32
        )
        weight = lax.dot_general(
            own_lane, x_hi[:, half:], TRANSPOSED_RIGHT, preferred_element_type=F32
        )[0:1, :]
        back = lax.dot_general(
            s["wd"][:, low], rows_of(s["glo"], g, every), TRANSPOSED_RIGHT, preferred_element_type=F32
        ) + lax.dot_general(
            s["wd"][:, high], rows_of(s["ghi"], g, every), TRANSPOSED_RIGHT, preferred_element_type=F32
        )
        pre_gate, pre_up = pre[:units], pre[units:]
        sigmoid = 1.0 / (1.0 + jnp.exp(-pre_gate))
        silu = pre_gate * sigmoid
        active = silu * pre_up
        total = jnp.sum(active * back, axis=0, keepdims=True)
        total = jnp.transpose(jnp.broadcast_to(total, (LANES, LANES)))
        s["scaled"][:, cols] = (weight * active).astype(BF16)
        weighted = weight * back
        s["dcat"][:units, cols] = (
            weighted * pre_up * sigmoid * (1.0 + pre_gate * (1.0 - sigmoid))
        ).astype(BF16)
        s["dcat"][units:, cols] = (weighted * silu).astype(BF16)
        rows = lax.dot_general(
            s["dcat"][:, cols], s["wgu"][...], TRANSPOSED_LEFT, preferred_element_type=F32
        )
        for i in range(pair):
            z = z_at(g * pair + i)
            part = slice(2 * CAP * i, 2 * CAP * (i + 1))
            at = pl.ds(2 * z, 2)
            mine_rows, mine_total = rows[part].reshape(2, CAP, dim), total[part].reshape(2, CAP, LANES)
            s["rfull"][at, :, :dim] = mine_rows
            s["rhalf"][at, :, :dim] = mine_rows.astype(BF16)
            s["rfull"][at, :, dim:] = mine_total
            s["rhalf"][at, :, dim:] = split(mine_total)
            crossing[g * pair + i] = send(s["rhalf"].at[2 * z + 1 - core], s["sib"].at[z], sibling)

    for load in loads:
        load.wait()
    for step in range(1, long):
        ring_step(x_low, step)
        ring_step(x_high, step)
        ring_step(g_low, step - 1)
        ring_step(g_high, step - 1)
        if step >= 2:
            compute(groups + 1 - step)
    compute(1)
    ring_step(g_low, long - 1)
    ring_step(g_high, long - 1)
    compute(0)

    tile = dim // 4

    def weights(n):
        cols = slice(n * tile, (n + 1) * tile)
        at = slice(n % 2 * tile, n % 2 * tile + tile)
        x_rows = jnp.concatenate([rows_at(s["xlo" if n < 2 else "xhi"], p, at) for p in range(nz)], axis=0)
        s["sums"][:, cols] = jnp.dot(s["dcat"][...], x_rows, preferred_element_type=F32)
        g_rows = jnp.concatenate([rows_at(s["glo" if n < 2 else "ghi"], p, at) for p in range(nz)], axis=0)
        s["sums_down"][:, cols] = jnp.dot(s["scaled"][...], g_rows, preferred_element_type=F32)

    sections = sections_of(dim)

    def piece(section, z):
        _, start, width, gate = section
        cols = slice(start, start + width)
        value = s["rfull"][2 * z + core, :, cols] + s["sib"][z, :, cols].astype(F32)
        if not gate:
            return value, None
        return value, s["rfull"][2 * z + core, :, dim:] + join(s["sib"][z, :, dim:])

    def add(value, ref, width):
        rows, gate_rows = value
        rows = rows + ref[:, :width].astype(F32)
        if gate_rows is not None:
            gate_rows = gate_rows + join(ref[:, width:])
        return rows, gate_rows

    crossed = set()

    def need(p):
        if p not in crossed:
            crossing[p].wait_recv()
            crossed.add(p)

    def place_of(distance):
        far = distance % nz - nz // 2
        return 2 * far if far >= 0 else -2 * far - 1

    last, first, second = {}, {}, {}

    def reduce_step(n, step):
        section = sections[n]
        hops = (long, short) if section[0] else (short, long)
        width = section[2]
        for side, sign in ((0, 1), (1, -1)):
            if step >= hops[side]:
                continue
            if step:
                last[n, side].wait_recv()
            distance = sign * (hops[side] - step)
            need(place_of(distance))
            value = piece(section, (mz + distance + nz) % nz)
            if step:
                value = add(value, s[f"got{n}"].at[side, step - 1], width)
            put = s[f"put{n}"].at[side, step]
            put[:, :width] = value[0].astype(BF16)
            if section[3]:
                put[:, width:] = split(value[1])
            last[n, side] = send(
                put, s[f"got{n}"].at[side, step], at_z(up_z if side == 0 else down_z)
            )

    def back_to_tokens(place, rows):
        return lax.dot_general(place, rows, TRANSPOSED_LEFT, preferred_element_type=F32).astype(BF16)

    def reduce_end(n):
        first_y, start, width, gate = section = sections[n]
        need(place_of(0))
        value = piece(section, mz)
        for side, hops in enumerate((long, short) if first_y else (short, long)):
            if hops:
                last[n, side].wait_recv()
                value = add(value, s[f"got{n}"].at[side, hops - 1], width)
        c, cr = s[f"c{n}"], s[f"cr{n}"]
        place = place_a if first_y else place_b
        c[:, :, :width] = back_to_tokens(place, value[0].astype(BF16)).reshape(c.shape[0], c.shape[1], width)
        if gate:
            lanes = lax.broadcasted_iota(jnp.int32, (CAP, LANES), 1)
            here = jnp.where(lanes % (LANES // 2) == mine, split(value[1]).astype(F32), 0.0).astype(BF16)
            c[:, :, width:] = back_to_tokens(place, here).reshape(c.shape[0], c.shape[1], LANES)
        if first_y:
            peers = [(my + d) % ny for d in sorted(range(1, ny), key=lambda d: -min(d, ny - d))]
            first[n] = [send(c.at[y], cr.at[my], at_y(y)) for y in peers]
            cr[my] = c[my]
        else:
            peers = [(mx + d) % nx for d in sorted(range(1, nx), key=lambda d: -min(d, nx - d))]
            first[n] = [send(c.at[x], cr.at[mx], at_x(x)) for x in peers]
            cr[mx] = c[mx]

    for turn in range(long + 1):
        for n in range(len(sections)):
            if turn < long:
                reduce_step(n, turn)
            else:
                reduce_end(n)
        if turn < 4:
            weights(turn)
        if turn == min(3, long):
            for n in range(turn + 1, 4):
                weights(n)
            stores = [
                pltpu.make_async_copy(s["sums"].at[pl.ds(0, units)], out_gate, s["lsem"].at[3]),
                pltpu.make_async_copy(s["sums"].at[pl.ds(units, units)], out_up, s["lsem"].at[4]),
                pltpu.make_async_copy(s["sums_down"], out_down, s["lsem"].at[5]),
            ]
            for store in stores:
                store.start()

    def total_of(buf):
        value = buf[0].astype(F32)
        for k in range(1, buf.shape[0]):
            value = value + buf[k].astype(F32)
        return value

    for n, section in enumerate(sections):
        arrive(first[n])
        e, er, wide = s[f"e{n}"], s[f"er{n}"], s[f"flat{n}"]
        wide[...] = total_of(s[f"cr{n}"])
        for k in range(e.shape[0]):
            e[k] = wide[2 * k : 2 * k + 2, :]
        if section[0]:
            peers = [(mx + d) % nx for d in sorted(range(1, nx), key=lambda d: -min(d, nx - d))]
            second[n] = [send(e.at[x], er.at[mx], at_x(x)) for x in peers]
            er[mx] = e[mx]
        else:
            peers = [(my + d) % ny for d in sorted(range(1, ny), key=lambda d: -min(d, ny - d))]
            second[n] = [send(e.at[y], er.at[my], at_y(y)) for y in peers]
            er[my] = e[my]

    for n, (_, start, width, gate) in enumerate(sections):
        arrive(second[n])
        final = total_of(s[f"er{n}"])
        out_in[:, start : start + width] = final[:, :width]
        if gate:
            grads = join(final[:, width:])
            inner = jnp.sum(spread * grads, axis=-1, keepdims=True)
            place = lax.broadcasted_iota(jnp.int32, (2, top), 1)
            result = jnp.zeros((2, top), F32)
            for k in range(top):
                own = jnp.sum(jnp.where(hits[k], grads, 0.0), axis=-1, keepdims=True)
                result = result + jnp.where(place == k, probs[:, k : k + 1] * (own - inner), 0.0)
            out_logits[...] = result
    for store in stores:
        store.wait()
    for copy in pending:
        copy.wait_send()


def hand_over(*refs):
    count = 5
    sources, results, stages = refs[:count], refs[count : 2 * count], refs[2 * count : 3 * count]
    load_sem, store_sem = refs[-2:]
    loads, stores = [], []
    for source, result, stage in zip(sources, results, stages):
        rows = source.shape[0]
        cuts = 6 if rows % 48 == 0 else 1
        for k in range(cuts):
            at, number = pl.ds(k * (rows // cuts), rows // cuts), len(loads)
            loads.append(pltpu.make_async_copy(source.at[at], stage.at[at], load_sem.at[number]))
            stores.append(pltpu.make_async_copy(stage.at[at], result.at[at], store_sem.at[number]))
    for load in loads:
        load.start()
    for load, store in zip(loads, stores):
        load.wait()
        store.start()
    for store in stores:
        store.wait()


def on_device(nx, ny, nz, tokens, grad_out, expert_ids, router_logits, w_gate, w_up, w_down):
    dim, units = w_gate.shape[1], w_gate.shape[2]
    shapes = scratch_of(nx, ny, nz, dim, units)
    spec = pl.BlockSpec(memory_space=pltpu.VMEM)
    anywhere = pl.BlockSpec(memory_space=pl.ANY)
    out_shape = [
        jax.ShapeDtypeStruct((2, dim), F32),
        jax.ShapeDtypeStruct(expert_ids.shape[1:], F32),
        jax.ShapeDtypeStruct((units, dim), F32),
        jax.ShapeDtypeStruct((units, dim), F32),
        jax.ShapeDtypeStruct((units, dim), F32),
    ]
    results = pl.pallas_call(
        functools.partial(kernel, nx, ny, nz, tuple(shapes)),
        out_shape=out_shape,
        in_specs=[spec] * 4 + [anywhere] * 3,
        out_specs=[spec] * 2 + [anywhere] * 3,
        scratch_shapes=list(shapes.values()),
        compiler_params=pltpu.CompilerParams(
            collective_id=0, has_side_effects=True, vmem_limit_bytes=56 * 1024 * 1024
        ),
    )(
        tokens[0], grad_out[0], expert_ids[0], router_logits[0],
        jnp.swapaxes(w_gate[0], 0, 1), jnp.swapaxes(w_up[0], 0, 1), w_down[0],
    )
    rows, logit_grads, sum_gate, sum_up, sum_down = pl.pallas_call(
        hand_over,
        out_shape=out_shape,
        in_specs=[anywhere] * 5,
        out_specs=[anywhere] * 5,
        scratch_shapes=[pltpu.VMEM(one.shape, F32) for one in out_shape]
        + [pltpu.SemaphoreType.DMA((20,))] * 2,
    )(*results)
    return (
        rows[None],
        logit_grads[None],
        jnp.swapaxes(sum_gate, 0, 1)[None],
        jnp.swapaxes(sum_up, 0, 1)[None],
        sum_down[None],
    )


def solution(mesh):
    side = math.isqrt(mesh.shape["expert"])
    nz = mesh.shape["hidden"] // 2
    token_spec, wide, tall = P("hidden", "expert", None), P("expert", None, "hidden"), P("expert", "hidden", None)
    return jax.shard_map(
        functools.partial(on_device, side, side, nz),
        mesh=mesh,
        in_specs=(token_spec,) * 4 + (wide, wide, tall),
        out_specs=(token_spec, token_spec, wide, wide, tall),
        check_vma=False,
    )
```
